32 devices in a mesh: dp: 2 (over y), ep: 4 (over x, core), tp: 4 (over z).
Axes of the slice: x: 2, y: 2, z: 4, core: 2. Of those that a mesh axis runs over, the one named last changes fastest.
Arguments:
- layer_input: bfloat16 [4096, 2048], P(('dp', 'ep', 'tp')), may hold values from -6 to 6
- cotangent: bfloat16 [4096, 2048], P(('dp', 'ep', 'tp')), may hold values from -6 to 6
- lengths: int32 [8], replicated, may hold values from 256 to 512, as said below
- seq_order: int32 [8], replicated, may hold values from 0 to 7, each once
- routes: int32 [4096, 4], P(('dp', 'ep')), may hold values from 0 to 7, all different within a row; in each aligned block of 512 rows (0 to 511, 512 to 1023, ...) at most 384 rows name the same one
- query_weight: bfloat16 [2048, 2048], P(('dp', 'ep'), 'tp'), may hold values from -0.125 to 0.125
- key_weight: bfloat16 [2048, 2048], P(('dp', 'ep'), 'tp'), may hold values from -0.125 to 0.125
- value_weight: bfloat16 [2048, 2048], P(('dp', 'ep'), 'tp'), may hold values from -0.125 to 0.125
- mixing_weight: bfloat16 [2048, 2048], P('tp', ('dp', 'ep')), may hold values from -0.5 to 0.5
- heads_bias: bfloat16 [3, 16, 128], P(None, 'tp', ('dp', 'ep')), may hold values from -3 to 3
- entry_gain: bfloat16 [2048], P(('dp', 'ep')), may hold values from 0.099609375 to 1.8984375
- middle_gain: bfloat16 [2048], P(('dp', 'ep')), may hold values from 0.099609375 to 1.8984375
- router_weight: bfloat16 [2048, 8], P(('dp', 'ep')), may hold values from -0.0625 to 0.0625
- shared_switch: bfloat16 [2048], P(('dp', 'ep')), may hold values from -0.125 to 0.125
- shared_gate: bfloat16 [2048, 5632], P(('dp', 'ep'), 'tp'), may hold values from -0.125 to 0.125
- shared_up: bfloat16 [2048, 5632], P(('dp', 'ep'), 'tp'), may hold values from -0.125 to 0.125
- shared_down: bfloat16 [5632, 2048], P('tp', ('dp', 'ep')), may hold values from -0.15625 to 0.15625
- expert_gate: bfloat16 [8, 2048, 1408], P('ep', None, 'tp'), may hold values from -0.125 to 0.125
- expert_up: bfloat16 [8, 2048, 1408], P('ep', None, 'tp'), may hold values from -0.125 to 0.125
- expert_down: bfloat16 [8, 1408, 2048], P('ep', 'tp'), may hold values from -1.25 to 1.25
Outputs:
- layer_output: bfloat16 [4096, 2048], P(('dp', 'ep', 'tp'))
- input_gradient: float32 [4096, 2048], P(('dp', 'ep', 'tp'))
- query_gradient: float32 [2048, 2048], P(('dp', 'ep'), 'tp')
- key_gradient: float32 [2048, 2048], P(('dp', 'ep'), 'tp')
- value_gradient: float32 [2048, 2048], P(('dp', 'ep'), 'tp')
- mixing_gradient: float32 [2048, 2048], P('tp', ('dp', 'ep'))
- bias_gradient: float32 [3, 16, 128], P(None, 'tp', ('dp', 'ep'))
- entry_gradient: float32 [2048], P(('dp', 'ep'))
- middle_gradient: float32 [2048], P(('dp', 'ep'))
- router_gradient: float32 [2048, 8], P(('dp', 'ep'))
- switch_gradient: float32 [2048], P(('dp', 'ep'))
- shared_gate_gradient: float32 [2048, 5632], P(('dp', 'ep'), 'tp')
- shared_up_gradient: float32 [2048, 5632], P(('dp', 'ep'), 'tp')
- shared_down_gradient: float32 [5632, 2048], P('tp', ('dp', 'ep'))
- expert_gate_gradient: float32 [8, 2048, 1408], P('ep', None, 'tp')
- expert_up_gradient: float32 [8, 2048, 1408], P('ep', None, 'tp')
- expert_down_gradient: float32 [8, 1408, 2048], P('ep', 'tp')
The draws below stay inside these ranges and needn't reach their ends.
Inputs may be any that keep to these rules, and one draw needn't show every extreme that they name: `lengths`: some sequence has exactly 512 tokens. `seq_order`: each group receives exactly one sequence. `routes`: the 4 experts of a row differ. In the rows of each group (aligned blocks of 512 rows) no expert is named more than 384 times, a bound that some block reaches.
All inputs are finite; a program needn't handle non-finite values.
Results may differ from the reference program's by a relative error of at most 0.04.
Values may be sent and summed in bfloat16 or wider, within the bound.
No kernel may reach another device: no remote copies, remote signals or barrier semaphores. Data moves between devices by JAX's collectives and lax.ppermute only.
A program may use at most 320 MiB of HBM per device.

```python
import math
import jax
import jax.numpy as jnp
import numpy as np
from jax import lax

D = 2048
NH = 16
HD = 128
FS = 5632
FE = 1408
TOP = 4
GROUP = 512
GROUPS = 8
TOKENS = 4096
EXPERTS = 8
CAP = 384
N_TP = 4


def draw_lengths(key, part):
    values = jax.random.randint(key, (GROUPS,), GROUP // 2, GROUP + 1)
    longest = jax.random.randint(jax.random.fold_in(key, 7), (), 0, GROUPS)
    return jnp.where(jnp.arange(GROUPS) == longest, GROUP, values).astype(jnp.int32)


def block_scale(rng, shape, shards, low, top_value):
    loudness = 1.0
    for axis_at, parts in shards:
        heights = jax.random.uniform(jax.random.fold_in(jax.random.fold_in(rng, 6), axis_at), (parts,), jnp.float32, low / len(shards), top_value / len(shards))
        loudness = loudness * jnp.repeat(jnp.exp(heights), shape[axis_at] // parts).reshape((-1,) + (1,) * (len(shape) - 1 - axis_at))
    return loudness


def deal_out(stream_key, own, number, rows, count, top, limit, skew):
    ranking = jax.random.permutation(stream_key, count)
    packed, ordinary = load_shares(count, rows * top, limit, skew, True), load_shares(count, rows * top, limit, skew, False)
    places = jnp.arange(count)

    def named(tallies, offset_by):
        used = int((tallies > 0).sum())
        fixed = max(1, used // 4)
        passed = fixed + (places - fixed + offset_by * (used - fixed)) % max(1, count - fixed)
        return jnp.zeros((count,), jnp.int32).at[ranking[jnp.where(places < fixed, places, passed)]].set(jnp.asarray(tallies, jnp.int32))

    tallies = jnp.where(number % 4 == 0, named(packed, number // 4), named(ordinary, number - number // 4 - 1))
    mixed = jax.random.permutation(jax.random.fold_in(own, 3), count)
    giver, taker = mixed[0:count // 2 * 2:2], mixed[1:count // 2 * 2:2]
    slack = jnp.minimum(tallies[giver] - 1, limit - tallies[taker]) // 2
    slack = jnp.where((giver == ranking[0]) | (taker == ranking[0]) | (tallies[taker] == 0), 0, jnp.maximum(slack, 0))
    passed = jax.random.randint(jax.random.fold_in(own, 4), (count // 2,), 0, 1 << 20) % (slack + 1)
    tallies = tallies.at[giver].add(-passed).at[taker].add(passed)
    labels = jnp.searchsorted(jnp.cumsum(tallies), jnp.arange(rows * top), side="right").astype(jnp.int32)
    grid = labels.reshape(top, rows).T
    grid = grid[jax.random.permutation(jax.random.fold_in(own, 1), rows)]
    offset_by = jax.random.randint(jax.random.fold_in(own, 2), (rows, 1), 0, top)
    return jnp.take_along_axis(grid, (jnp.arange(top)[None, :] + offset_by) % top, axis=1)


def load_shares(count, total, bound, lean, full):
    loads = [(1 << 20) // math.isqrt(rank ** lean) + 1 for rank in range(1, count + 1)]
    largest = bound if full else min(bound, max(-(-total // count), total * loads[0] // sum(loads)))
    least = 1 if total - largest >= count - 1 else 0
    holding, rest = [largest] + [least] * (count - 1), total - largest - least * (count - 1)
    while rest > 0:
        movable = [i for i in range(1, count) if holding[i] < largest] or [i for i in range(1, count) if holding[i] < bound]
        pool, remaining = sum([loads[i] for i in movable]), rest
        for i in movable:
            more = min(bound - holding[i], max(1, remaining * loads[i] // pool), rest)
            holding[i] = holding[i] + more
            rest = rest - more
    return np.array(holding)


def normal_values(own_key, dims, scale, reach, shards=(), held_as=jnp.bfloat16):
    entries = jax.random.normal(own_key, dims, jnp.float32) * scale
    if len(shards) > 0:
        entries = block_scale(own_key, dims, shards, -0.22, 0.18) * entries
    return jnp.clip(entries, min=-reach, max=reach).astype(held_as)


def setup_inputs(seed: int = 0) -> dict:
    streams_of = jax.random.split(jax.random.key(seed), 21)
    layer_input = normal_values(streams_of[0], (TOKENS, D), 1.0, 6.0, ((0, 32),))
    cotangent = normal_values(streams_of[1], (TOKENS, D), 1.0, 6.0, ((0, 32),))
    lengths = draw_lengths(jax.random.fold_in(streams_of[20], 71), 0)
    seq_order = jax.random.permutation(streams_of[3], GROUPS).astype(jnp.int32)
    routes_keys = jax.random.split(jax.random.fold_in(streams_of[4], 1), TOKENS // GROUP)
    routes_turns = jax.random.permutation(jax.random.fold_in(streams_of[4], 3), TOKENS // GROUP)
    routes = jax.vmap(lambda own, number: deal_out(jax.random.fold_in(streams_of[4], 2), own, number, GROUP, EXPERTS, TOP, CAP, 1))(routes_keys, routes_turns).reshape((TOKENS, TOP))
    query_weight = normal_values(streams_of[5], (D, D), D ** -0.5, 0.125, ((0, 8), (1, 4)))
    key_weight = normal_values(streams_of[6], (D, D), D ** -0.5, 0.125, ((0, 8), (1, 4)))
    value_weight = normal_values(streams_of[7], (D, D), D ** -0.5, 0.125, ((0, 8), (1, 4)))
    mixing_weight = normal_values(streams_of[8], (D, D), (D // 16) ** -0.5, 0.5, ((0, 4), (1, 8)))
    heads_bias = normal_values(streams_of[9], (3, NH, HD), 0.5, 3.0, ((1, 4), (2, 8)))
    entry_gain = jnp.clip(1.0 + 0.18 * jax.random.normal(streams_of[10], (D,), jnp.float32), 0.099609375, 1.8984375).astype(jnp.bfloat16)
    middle_gain = jnp.clip(1.0 + 0.18 * jax.random.normal(streams_of[11], (D,), jnp.float32), 0.099609375, 1.8984375).astype(jnp.bfloat16)
    router_weight = normal_values(streams_of[12], (D, EXPERTS), (4 * D) ** -0.5, 0.0625, ((0, 8),))
    shared_switch = normal_values(streams_of[13], (D,), D ** -0.5, 0.125, ((0, 8),))
    shared_gate = normal_values(streams_of[14], (D, FS), D ** -0.5, 0.125, ((0, 8), (1, 4)))
    shared_up = normal_values(streams_of[15], (D, FS), D ** -0.5, 0.125, ((0, 8), (1, 4)))
    shared_down = normal_values(streams_of[16], (FS, D), (FS // 4) ** -0.5, 0.15625, ((0, 4), (1, 8)))
    expert_gate = normal_values(streams_of[17], (EXPERTS, D, FE), D ** -0.5, 0.125, ((0, 4), (2, 4)))
    expert_up = normal_values(streams_of[18], (EXPERTS, D, FE), D ** -0.5, 0.125, ((0, 4), (2, 4)))
    expert_down = normal_values(streams_of[19], (EXPERTS, FE, D), (FE // 64) ** -0.5, 1.25, ((0, 4), (1, 4)))
    return {"layer_input": layer_input, "cotangent": cotangent, "lengths": lengths, "seq_order": seq_order, "routes": routes, "query_weight": query_weight, "key_weight": key_weight, "value_weight": value_weight, "mixing_weight": mixing_weight, "heads_bias": heads_bias, "entry_gain": entry_gain, "middle_gain": middle_gain, "router_weight": router_weight, "shared_switch": shared_switch, "shared_gate": shared_gate, "shared_up": shared_up, "shared_down": shared_down, "expert_gate": expert_gate, "expert_up": expert_up, "expert_down": expert_down}


EPS = 1e-06
THETA = 1000000.0

@jax.custom_vjp
def low(v):
    return lax.optimization_barrier(v.astype(jnp.bfloat16)).astype(jnp.float32)

@jax.custom_vjp
def low_back(v):
    return v

def low_keep(v):
    return (low(v), None)

def low_pass(kept, grad):
    return (grad,)

def back_keep(v):
    return (v, None)

def back_low(kept, grad):
    return (low(grad),)
low.defvjp(low_keep, low_pass)
low_back.defvjp(back_keep, back_low)

def matmul_high(left, right):
    return jnp.dot(left, right, precision=lax.Precision.HIGHEST)

def unit_norm(values):
    return values * lax.rsqrt(lax.optimization_barrier(jnp.mean(values * values, axis=-1, keepdims=True)) + EPS)

def rotate(values):
    middle = values.shape[-1] // 2
    return jnp.concatenate([-values[..., middle:], values[..., :middle]], axis=-1)

def rope_tables(row_total):
    position = jnp.arange(row_total).astype(jnp.float32)
    freqs = THETA ** (-(jnp.arange(HD // 2).astype(jnp.float32) * 2.0) / HD)
    angles = position[:, None] * freqs[None, :]
    angles = jnp.concatenate([angles, angles], axis=-1)
    return (jnp.cos(angles)[:, None, :], jnp.sin(angles)[:, None, :])

def expert_rows(normed, gate_matrix, up_matrix, down_matrix):
    block_width = FE // N_TP
    summed = jnp.zeros((normed.shape[0], D), jnp.float32)
    for block_number in range(N_TP):
        start = block_number * block_width
        block_input = low_back(normed)
        pre_gate = low_back(matmul_high(block_input, gate_matrix[:, start:start + block_width]))
        pre_up = low_back(matmul_high(block_input, up_matrix[:, start:start + block_width]))
        hidden_low = low(jax.nn.silu(pre_gate) * pre_up)
        summed = summed + low(matmul_high(hidden_low, down_matrix[start:start + block_width, :]))
    return low_back(summed)

def group_layer(weights, group_input, group_routes, group_length):
    query_full, key_full, value_full, mixing_full, bias_full, entry_full, middle_full, router_full, switch_full, gate_full, up_full, down_full, expert_gates, expert_ups, expert_downs = weights
    row_ids = jnp.arange(GROUP)
    row_keep = (row_ids < group_length).astype(jnp.float32)
    entry_normed = low(unit_norm(group_input) * entry_full)
    query_lin = low_back(matmul_high(entry_normed, query_full) + bias_full[0].reshape(D))
    key_lin = low_back(matmul_high(entry_normed, key_full) + bias_full[1].reshape(D))
    value_lin = matmul_high(entry_normed, value_full) + bias_full[2].reshape(D)
    cosine, sine = rope_tables(GROUP)
    query_heads = query_lin.reshape(GROUP, NH, HD)
    key_heads = key_lin.reshape(GROUP, NH, HD)
    query_rot = low(query_heads * cosine + rotate(query_heads) * sine)
    key_rot = low(key_heads * cosine + rotate(key_heads) * sine)
    value_heads = low(low_back(value_lin)).reshape(GROUP, NH, HD)
    scores = jnp.einsum('qhd,khd->hqk', query_rot, key_rot, precision=lax.Precision.HIGHEST) * HD ** (-0.5)
    scores = low_back(scores)
    causal = row_ids[:, None] >= row_ids[None, :]
    scores = jnp.where(causal[None], scores, -1e+30)
    probs_low = low(jax.nn.softmax(scores, axis=-1))
    context = jnp.einsum('hqk,khd->qhd', probs_low, value_heads, precision=lax.Precision.HIGHEST)
    context_low = low(low_back(context)).reshape(GROUP, D)
    attention = low_back(matmul_high(context_low, mixing_full))
    hidden_state = group_input + row_keep[:, None] * attention
    normed = low(unit_norm(hidden_state) * middle_full)
    expert_probs = jax.nn.softmax(matmul_high(normed, router_full), axis=-1)
    route_picks = (group_routes[:, :, None] == jnp.arange(EXPERTS)[None, None, :]).astype(jnp.float32)
    route_gates = row_keep[:, None] * lax.optimization_barrier(jnp.sum(expert_probs[:, None, :] * route_picks, axis=-1))
    switch_value = jax.nn.sigmoid(matmul_high(normed, switch_full))
    shared_pre_gate = low_back(matmul_high(normed, gate_full))
    shared_pre_up = low_back(matmul_high(normed, up_full))
    shared_hidden = low(jax.nn.silu(shared_pre_gate) * shared_pre_up)
    shared_out = low_back(matmul_high(shared_hidden, down_full))
    expert_weights = lax.optimization_barrier(jnp.sum(route_gates[:, :, None] * route_picks, axis=1))
    expert_outs = lax.map(lambda stacked: expert_rows(normed, stacked[0], stacked[1], stacked[2]), (expert_gates, expert_ups, expert_downs))
    routed = jnp.einsum('te,etd->td', expert_weights, expert_outs, precision=lax.Precision.HIGHEST)
    return hidden_state + (row_keep * switch_value)[:, None] * shared_out + routed

def reference(layer_input, cotangent, lengths, seq_order, routes, query_weight, key_weight, value_weight, mixing_weight, heads_bias, entry_gain, middle_gain, router_weight, shared_switch, shared_gate, shared_up, shared_down, expert_gate, expert_up, expert_down):
    group_lengths = jnp.take(lengths, seq_order)
    weights = tuple((item.astype(jnp.float32) for item in (query_weight, key_weight, value_weight, mixing_weight, heads_bias, entry_gain, middle_gain, router_weight, shared_switch, shared_gate, shared_up, shared_down, expert_gate, expert_up, expert_down)))
    route_groups = routes.reshape(GROUPS, GROUP, TOP)
    layer_step = jax.checkpoint(group_layer)

    def forward(params, inputs):
        blocks = inputs.reshape(GROUPS, GROUP, D)
        outputs = lax.map(lambda stacked: layer_step(params, stacked[0], stacked[1], stacked[2]), (blocks, route_groups, group_lengths))
        return outputs.reshape(TOKENS, D)
    result, pullback = jax.vjp(forward, weights, layer_input.astype(jnp.float32))
    weight_grads, input_grads = pullback(cotangent.astype(jnp.float32))
    return (result.astype(jnp.bfloat16), input_grads, weight_grads[0], weight_grads[1], weight_grads[2], weight_grads[3], weight_grads[4], weight_grads[5], weight_grads[6], weight_grads[7], weight_grads[8], weight_grads[9], weight_grads[10], weight_grads[11], weight_grads[12], weight_grads[13], weight_grads[14])
```

```python
import jax
import jax.numpy as jnp
from jax import lax
from jax.sharding import PartitionSpec as P

HD = 128
TOP = 4
EPS = 1e-06
THETA = 1000000.0
LANES = 128
F32 = jnp.float32
BF16 = jnp.bfloat16


def dot_nn(left, right):
    return lax.dot_general(left, right, (((1,), (0,)), ((), ())), preferred_element_type=F32)


def dot_nt(left, right):
    return lax.dot_general(left, right, (((1,), (1,)), ((), ())), preferred_element_type=F32)


def dot_tn(left, right):
    return lax.dot_general(left, right, (((0,), (0,)), ((), ())), preferred_element_type=F32)


def dot_exact(left, right, dims):
    return lax.dot_general(
        left, right, (dims, ((), ())), precision=lax.Precision.HIGHEST, preferred_element_type=F32
    )


def norm_parts(values):
    inverse = lax.rsqrt(jnp.mean(values * values, axis=-1, keepdims=True) + EPS)
    return (values * inverse, inverse)


def norm_back(grad_normed, gain_vector, unit_rows, inverse):
    scaled = grad_normed * gain_vector
    return inverse * (scaled - unit_rows * jnp.mean(scaled * unit_rows, axis=-1, keepdims=True))


def rotate(values):
    middle = values.shape[-1] // 2
    return jnp.concatenate([-values[..., middle:], values[..., :middle]], axis=-1)


def unrotate(values):
    middle = values.shape[-1] // 2
    return jnp.concatenate([values[..., middle:], -values[..., :middle]], axis=-1)


def split_pair(values):
    high = values.astype(BF16)
    rest = values - lax.reduce_precision(values, exponent_bits=8, mantissa_bits=7)
    return high, rest.astype(BF16)


def shifted(block, axis, step):
    count = lax.axis_size(axis)
    return lax.ppermute(block, axis, [(i, (i + step) % count) for i in range(count)])


def gather_blocks(block, axis):
    count = lax.axis_size(axis)
    return [block] + [shifted(block, axis, step) for step in range(1, count)]


def scatter_blocks(blocks, axis):
    total = blocks[0]
    for step in range(1, len(blocks)):
        total = total + shifted(blocks[step].astype(BF16), axis, -step).astype(F32)
    return total


def exchange_sum(values, axis):
    count = lax.axis_size(axis)
    if count & (count - 1):
        return lax.psum(values, axis)
    bit = 1
    while bit < count:
        values = values + lax.ppermute(values, axis, [(i, i ^ bit) for i in range(count)])
        bit *= 2
    return values


def whole_sum(values, axis):
    if lax.axis_size(axis) == 2:
        other = lax.ppermute(values, axis, [(0, 1), (1, 0)])
        return values.astype(F32) + other.astype(F32)
    return lax.psum(values, axis).astype(F32)


def shard_sum(values, axis):
    if lax.axis_size(axis) == 2:
        place = lax.axis_index(axis)
        other = lax.ppermute(
            lax.dynamic_index_in_dim(values, 1 - place, 0, False), axis, [(0, 1), (1, 0)]
        )
        return lax.dynamic_index_in_dim(values, place, 0, False).astype(F32) + other.astype(F32)
    return lax.psum_scatter(values, axis, scatter_dimension=0, tiled=False).astype(F32)


def pair_gather(values, axis):
    if lax.axis_size(axis) == 2:
        place = lax.axis_index(axis)
        other = lax.ppermute(values, axis, [(0, 1), (1, 0)])
        first = jnp.where(place == 0, values, other)
        second = jnp.where(place == 0, other, values)
        return jnp.stack([first, second])
    return lax.all_gather(values, axis)


def body(
    layer_input,
    cotangent,
    lengths,
    seq_order,
    routes,
    query_weight,
    key_weight,
    value_weight,
    mixing_weight,
    heads_bias,
    entry_gain,
    middle_gain,
    router_weight,
    shared_switch,
    shared_gate,
    shared_up,
    shared_down,
    expert_gate,
    expert_up,
    expert_down,
):
    tp_count = lax.axis_size("tp")
    ep_count = lax.axis_size("ep")
    dp_count = lax.axis_size("dp")
    part_count = dp_count * ep_count
    tp_index = lax.axis_index("tp")
    ep_index = lax.axis_index("ep")
    own_rows, width = layer_input.shape
    group_rows = own_rows * tp_count
    span_rows = group_rows * ep_count
    slice_rows = query_weight.shape[0]
    head_cols = query_weight.shape[1]
    head_count = head_cols // HD
    local_experts = expert_gate.shape[0]
    expert_count = router_weight.shape[1]
    hidden = expert_gate.shape[2]
    shared_hidden = shared_gate.shape[1] // ep_count
    segments = local_experts + 1
    seg = -(-max(hidden, shared_hidden) // LANES) * LANES

    group_index = lax.axis_index(("dp", "ep"))
    length = jnp.take(lengths, jnp.take(seq_order, group_index))
    own_keep = ((tp_index * own_rows + jnp.arange(own_rows)) < length).astype(F32)[:, None]
    block_of = jnp.arange(group_rows) // own_rows
    position = ((tp_index - block_of) % tp_count) * own_rows + jnp.arange(group_rows) % own_rows

    bias_rows = heads_bias.size
    small = jnp.concatenate(
        [
            router_weight,
            shared_switch[:, None],
            entry_gain[:, None],
            middle_gain[:, None],
        ],
        axis=1,
    )
    bias_depth = -(-bias_rows // slice_rows)
    bias_cols = jnp.pad(heads_bias.reshape(-1), (0, bias_depth * slice_rows - bias_rows))
    bias_cols = bias_cols.reshape(bias_depth, slice_rows).T
    small = jnp.concatenate([small, bias_cols], axis=1)
    small = jnp.pad(small, ((0, 0), (0, LANES - small.shape[1])))
    dense_own = jnp.concatenate(
        [query_weight, key_weight, value_weight, mixing_weight.T, small], axis=1
    )
    dense_full = lax.all_gather(dense_own, ("dp", "ep"), axis=0, tiled=True)
    in_weight = dense_full[:, : 3 * head_cols]
    out_weight = dense_full[:, 3 * head_cols : 4 * head_cols]
    small_full = dense_full[:, 4 * head_cols :]
    small_rows = small_full[:, : expert_count + 3].astype(F32).T
    entry_full = small_rows[expert_count + 1][None]
    middle_full = small_rows[expert_count + 2][None]
    bias_full = small_full[:, expert_count + 3 : expert_count + 3 + bias_depth]
    bias_full = bias_full.reshape(part_count, slice_rows, bias_depth).transpose(0, 2, 1)
    bias_full = bias_full.reshape(part_count, -1)[:, :bias_rows]
    bias_full = bias_full.reshape((part_count,) + heads_bias.shape).transpose(1, 2, 0, 3)
    bias_full = bias_full.reshape(1, 3 * head_cols).astype(F32)

    input_values = jnp.concatenate(gather_blocks(layer_input, "tp"), axis=0).astype(F32)
    entry_unit, entry_inverse = norm_parts(input_values)
    entry_normed = (entry_unit * entry_full).astype(BF16)

    def to_owners(matrix):
        return matrix.reshape(ep_count, shared_hidden, slice_rows)

    shared_own = jnp.concatenate(
        [to_owners(shared_gate.T), to_owners(shared_up.T), to_owners(shared_down)], axis=1
    )
    shared_span = lax.all_to_all(shared_own, "ep", split_axis=0, concat_axis=0, tiled=True)
    shared_parts = pair_gather(shared_span, "dp").reshape(
        part_count, 3, shared_hidden, slice_rows
    )
    shared_parts = shared_parts.transpose(1, 2, 0, 3).reshape(3, shared_hidden, width)

    def stack_hidden(expert_rows, shared_rows):
        padded = [jnp.pad(rows, ((0, seg - rows.shape[0]), (0, 0))) for rows in expert_rows]
        padded.append(jnp.pad(shared_rows, ((0, seg - shared_hidden), (0, 0))))
        return padded

    gate_rows = stack_hidden([expert_gate[j].T for j in range(local_experts)], shared_parts[0])
    up_rows = stack_hidden([expert_up[j].T for j in range(local_experts)], shared_parts[1])
    down_rows = stack_hidden([expert_down[j] for j in range(local_experts)], shared_parts[2])
    first_weight = jnp.concatenate(gate_rows + up_rows, axis=0)
    down_weight = jnp.concatenate(down_rows, axis=0)

    in_lin = dot_nn(entry_normed, in_weight) + bias_full
    freqs = THETA ** (-(jnp.arange(HD // 2).astype(F32) * 2.0) / HD)
    angles = position.astype(F32)[:, None] * freqs[None, :]
    angles = jnp.concatenate([angles, angles], axis=-1)
    cosine = jnp.cos(angles)[:, None, :]
    sine = jnp.sin(angles)[:, None, :]
    query_heads = in_lin[:, :head_cols].reshape(group_rows, head_count, HD)
    key_heads = in_lin[:, head_cols : 2 * head_cols].reshape(group_rows, head_count, HD)
    query_rot = (query_heads * cosine + rotate(query_heads) * sine).astype(BF16)
    key_rot = (key_heads * cosine + rotate(key_heads) * sine).astype(BF16)
    value_heads = in_lin[:, 2 * head_cols :].astype(BF16).reshape(group_rows, head_count, HD)
    score_scale = HD ** (-0.5)
    causal = position[:, None] >= position[None, :]

    def score_matrix():
        raw_scores = jnp.einsum("qhd,khd->hqk", query_rot, key_rot, preferred_element_type=F32)
        return jnp.where(causal[None], raw_scores * score_scale, -1e30)

    scores = score_matrix()
    top_score = jnp.max(scores, axis=-1, keepdims=True)
    log_total = top_score + jnp.log(jnp.sum(jnp.exp(scores - top_score), axis=-1, keepdims=True))
    attn_probs = jnp.exp(scores - log_total).astype(BF16)
    context = jnp.einsum("hqk,khd->qhd", attn_probs, value_heads, preferred_element_type=F32)
    context_low = context.astype(BF16).reshape(group_rows, head_cols)
    head_terms = dot_nt(context_low, out_weight)
    attention_own = scatter_blocks(
        [head_terms[j * own_rows : (j + 1) * own_rows] for j in range(tp_count)], "tp"
    )

    hidden_state = input_values[:own_rows] + own_keep * attention_own
    middle_unit, middle_inverse = norm_parts(hidden_state)
    middle_normed = (middle_unit * middle_full).astype(BF16)
    own_logits = dot_nn(middle_normed, small_full)
    expert_probs = jax.nn.softmax(own_logits[:, :expert_count], axis=-1)
    switch_value = jax.nn.sigmoid(own_logits[:, expert_count : expert_count + 1])
    own_routes = lax.dynamic_slice_in_dim(routes, tp_index * own_rows, own_rows, 0)
    route_mask = jnp.any(
        own_routes[:, :, None] == jnp.arange(expert_count)[None, None, :], axis=1
    ).astype(F32)
    row_gates = jnp.concatenate([own_keep * route_mask * expert_probs, own_keep * switch_value], axis=1)
    gate_high, gate_low = split_pair(row_gates)
    gate_cols = expert_count + 1
    half = LANES // 2
    extra = jnp.concatenate(
        [
            jnp.pad(gate_high, ((0, 0), (0, half - gate_cols))),
            jnp.pad(gate_low, ((0, 0), (0, half - gate_cols))),
        ],
        axis=1,
    )

    upstream = lax.all_gather(cotangent, ("ep", "tp"), axis=0, tiled=True)
    sent_rows = jnp.concatenate([middle_normed, extra], axis=1)
    span_all = lax.all_gather(sent_rows, ("ep", "tp"), axis=0, tiled=True)
    span_normed = span_all[:, :width]
    span_extra = span_all[:, width:].astype(F32)
    span_gates = span_extra[:, :half] + span_extra[:, half:]
    lane = jnp.arange(half)[None, :]
    gate_of = [
        jnp.sum(jnp.where(lane == ep_index * local_experts + j, span_gates, 0.0), axis=1, keepdims=True)
        for j in range(local_experts)
    ] + [span_gates[:, expert_count : expert_count + 1]]
    gate_wide = jnp.concatenate(
        [jnp.broadcast_to(column, (span_rows, seg)) for column in gate_of], axis=1
    )

    first_lin = dot_nt(span_normed, first_weight)
    pre_gate = first_lin[:, : segments * seg]
    pre_up = first_lin[:, segments * seg :]
    sigmoid = jax.nn.sigmoid(pre_gate)
    act = pre_gate * sigmoid
    slope = sigmoid * (1.0 + pre_gate * (1.0 - sigmoid))
    hidden_low = (act * pre_up).astype(BF16)
    hidden_gated = (gate_wide * hidden_low.astype(F32)).astype(BF16)
    back_lin = dot_nt(upstream, down_weight)
    gate_terms = hidden_low.astype(F32) * back_lin
    gate_parts = jnp.concatenate(
        [
            jnp.sum(gate_terms[:, j * seg : (j + 1) * seg], axis=1, keepdims=True)
            for j in range(segments)
        ],
        axis=1,
    )
    hidden_grad = gate_wide * back_lin
    gate_grad_low = (hidden_grad * pre_up * slope).astype(BF16)
    up_grad_low = (hidden_grad * act).astype(BF16)
    first_grad = jnp.concatenate([gate_grad_low, up_grad_low], axis=1)

    normed_part = dot_nn(first_grad, first_weight).astype(BF16)
    column_of = jnp.concatenate(
        [ep_index * local_experts + jnp.arange(local_experts), jnp.array([expert_count])]
    )
    part_place = (column_of[:, None] == jnp.arange(half)[None, :]).astype(F32)
    placed = jnp.sum(gate_parts[:, :, None] * part_place[None], axis=1)
    placed_high, placed_low = split_pair(placed)
    back_rows = jnp.concatenate([normed_part, placed_high, placed_low], axis=1)
    back_own = lax.psum_scatter(back_rows, ("ep", "tp"), scatter_dimension=0, tiled=True).astype(F32)
    branch = dot_nn(hidden_gated, down_weight).astype(BF16)
    branch_own = lax.psum_scatter(branch, ("ep", "tp"), scatter_dimension=0, tiled=True).astype(F32)
    layer_output = (hidden_state + branch_own).astype(BF16)

    down_grad = dot_tn(hidden_gated, upstream).astype(BF16)
    first_weight_grad = dot_tn(first_grad, span_normed).astype(BF16)

    def segment_rows(matrix, place, count):
        return matrix[place * seg : place * seg + count]

    expert_first = jnp.concatenate(
        [segment_rows(first_weight_grad, j, hidden) for j in range(local_experts)]
        + [segment_rows(first_weight_grad, segments + j, hidden) for j in range(local_experts)],
        axis=0,
    )
    expert_last = jnp.concatenate(
        [segment_rows(down_grad, j, hidden) for j in range(local_experts)], axis=0
    )
    expert_last_sum = whole_sum(expert_last, "dp").reshape(local_experts, hidden, width)
    expert_first_sum = whole_sum(expert_first, "dp").reshape(2, local_experts, hidden, width)
    shared_grad = jnp.concatenate(
        [
            segment_rows(first_weight_grad, local_experts, shared_hidden),
            segment_rows(first_weight_grad, segments + local_experts, shared_hidden),
            segment_rows(down_grad, local_experts, shared_hidden),
        ],
        axis=0,
    )
    shared_grad = shared_grad.reshape(3 * shared_hidden, dp_count, ep_count, slice_rows)
    shared_grad = shared_grad.transpose(1, 2, 0, 3)
    shared_mine = shard_sum(shared_grad, "dp").astype(BF16)
    shared_back = lax.all_to_all(shared_mine, "ep", split_axis=0, concat_axis=0, tiled=True)
    shared_back = shared_back.reshape(ep_count, 3, shared_hidden, slice_rows).astype(F32)

    normed_own = back_own[:, :width]
    gate_sums = back_own[:, width : width + half] + back_own[:, width + half :]
    prob_grad = own_keep * route_mask * gate_sums[:, :expert_count]
    logit_grad = expert_probs * (
        prob_grad - jnp.sum(expert_probs * prob_grad, axis=-1, keepdims=True)
    )
    switch_grad = (
        own_keep
        * gate_sums[:, expert_count : expert_count + 1]
        * switch_value
        * (1.0 - switch_value)
    )
    score_grad = jnp.concatenate([logit_grad, switch_grad], axis=1)
    normed_total = normed_own + dot_exact(score_grad, small_rows[: expert_count + 1], ((1,), (0,)))
    router_part = dot_exact(score_grad, middle_normed.astype(F32), ((0,), (0,)))
    middle_part = jnp.sum(normed_total * middle_unit, axis=0, keepdims=True)
    state_grad = cotangent.astype(F32) + norm_back(
        normed_total, middle_full, middle_unit, middle_inverse
    )
    attention_grad_own = (own_keep * state_grad).astype(BF16)
    attention_grad = jnp.concatenate(gather_blocks(attention_grad_own, "tp"), axis=0)

    mixing_grad = dot_tn(attention_grad, context_low)
    context_grad = dot_nn(attention_grad, out_weight)
    context_grad = context_grad.astype(BF16).reshape(group_rows, head_count, HD)
    probs_again = jnp.exp(score_matrix() - log_total)
    probs_low = probs_again.astype(BF16)
    value_grad = jnp.einsum("hqk,qhd->khd", probs_low, context_grad, preferred_element_type=F32)
    value_grad = value_grad.astype(BF16).reshape(group_rows, head_cols)
    prob_grads = jnp.einsum("qhd,khd->hqk", context_grad, value_heads, preferred_element_type=F32)
    row_delta = jnp.sum(probs_again * prob_grads, axis=-1, keepdims=True)
    score_grads = (probs_again * (prob_grads - row_delta)).astype(BF16)
    query_rot_grad = (
        jnp.einsum("hqk,khd->qhd", score_grads, key_rot, preferred_element_type=F32) * score_scale
    )
    key_rot_grad = (
        jnp.einsum("hqk,qhd->khd", score_grads, query_rot, preferred_element_type=F32) * score_scale
    )
    query_grad = (query_rot_grad * cosine + unrotate(query_rot_grad * sine)).astype(BF16)
    key_grad = (key_rot_grad * cosine + unrotate(key_rot_grad * sine)).astype(BF16)
    in_grad = jnp.concatenate(
        [query_grad.reshape(group_rows, head_cols), key_grad.reshape(group_rows, head_cols), value_grad],
        axis=1,
    )
    bias_grad = jnp.sum(in_grad.astype(F32), axis=0)
    entry_part = dot_nt(in_grad, in_weight)
    entry_own = scatter_blocks(
        [entry_part[j * own_rows : (j + 1) * own_rows] for j in range(tp_count)], "tp"
    )
    input_gradient = state_grad + norm_back(
        entry_own, entry_full, entry_unit[:own_rows], entry_inverse[:own_rows]
    )

    entry_gain_part = jnp.sum(entry_part * entry_unit, axis=0, keepdims=True)
    small_part = exchange_sum(
        jnp.concatenate([router_part, entry_gain_part, middle_part], axis=0), "tp"
    )
    bias_part = bias_grad.reshape(3, head_count, part_count, -1).transpose(2, 0, 1, 3)
    bias_part = bias_part.reshape(part_count, bias_rows)
    bias_part = jnp.pad(bias_part, ((0, 0), (0, bias_depth * slice_rows - bias_rows)))
    bias_part = bias_part.reshape(part_count, bias_depth, slice_rows).transpose(1, 0, 2)
    bias_part = bias_part.reshape(bias_depth, width)
    small_part = jnp.concatenate([small_part, bias_part], axis=0)
    small_high, small_low = split_pair(small_part)
    small_count = small_part.shape[0]
    small_cols = jnp.concatenate(
        [
            jnp.pad(small_high, ((0, half - small_count), (0, 0))),
            jnp.pad(small_low, ((0, half - small_count), (0, 0))),
        ],
        axis=0,
    ).T
    dense_grad = jnp.concatenate(
        [
            dot_tn(entry_normed, in_grad).astype(BF16),
            mixing_grad.astype(BF16),
            small_cols,
        ],
        axis=1,
    )
    dense_sum = lax.psum_scatter(
        dense_grad, ("dp", "ep"), scatter_dimension=0, tiled=True
    ).astype(F32)
    small_sum = dense_sum[:, 4 * head_cols : 4 * head_cols + half] + dense_sum[:, 4 * head_cols + half :]
    bias_sum = small_sum[:, expert_count + 3 : expert_count + 3 + bias_depth]
    bias_sum = bias_sum.T.reshape(-1)[:bias_rows].reshape(heads_bias.shape)

    def by_columns(rows):
        return rows.transpose(2, 0, 1).reshape(slice_rows, ep_count * shared_hidden)

    return (
        layer_output,
        input_gradient,
        dense_sum[:, :head_cols],
        dense_sum[:, head_cols : 2 * head_cols],
        dense_sum[:, 2 * head_cols : 3 * head_cols],
        dense_sum[:, 3 * head_cols : 4 * head_cols].T,
        bias_sum,
        small_sum[:, expert_count + 1],
        small_sum[:, expert_count + 2],
        small_sum[:, :expert_count],
        small_sum[:, expert_count],
        by_columns(shared_back[:, 0]),
        by_columns(shared_back[:, 1]),
        shared_back[:, 2].reshape(ep_count * shared_hidden, slice_rows),
        expert_first_sum[0].transpose(0, 2, 1),
        expert_first_sum[1].transpose(0, 2, 1),
        expert_last_sum,
    )


def solution(mesh):
    rows = P(("dp", "ep", "tp"), None)
    parts = P(("dp", "ep"))
    in_cols = P(("dp", "ep"), "tp")
    out_cols = P("tp", ("dp", "ep"))
    weights = (
        in_cols,
        in_cols,
        in_cols,
        out_cols,
        P(None, "tp", ("dp", "ep")),
        parts,
        parts,
        P(("dp", "ep"), None),
        parts,
        in_cols,
        in_cols,
        out_cols,
        P("ep", None, "tp"),
        P("ep", None, "tp"),
        P("ep", "tp", None),
    )
    return jax.shard_map(
        body,
        mesh=mesh,
        in_specs=(rows, rows, P(), P(), P(("dp", "ep"), None)) + weights,
        out_specs=(rows, rows) + weights,
        check_vma=False,
    )
```

```python
import jax
import jax.numpy as jnp
from jax import lax
from jax.experimental import pallas as pl
from jax.experimental.pallas import tpu as pltpu
from jax.sharding import PartitionSpec as P

HD = 128
TOP = 4
EPS = 1e-06
THETA = 1000000.0
LANES = 128
F32 = jnp.float32
BF16 = jnp.bfloat16


def dot_nn(left, right):
    return lax.dot_general(left, right, (((1,), (0,)), ((), ())), preferred_element_type=F32)


def dot_nt(left, right):
    return lax.dot_general(left, right, (((1,), (1,)), ((), ())), preferred_element_type=F32)


def dot_tn(left, right):
    return lax.dot_general(left, right, (((0,), (0,)), ((), ())), preferred_element_type=F32)


def dot_exact(left, right, dims):
    return lax.dot_general(
        left, right, (dims, ((), ())), precision=lax.Precision.HIGHEST, preferred_element_type=F32
    )


def norm_parts(values):
    inverse = lax.rsqrt(jnp.mean(values * values, axis=-1, keepdims=True) + EPS)
    return (values * inverse, inverse)


def norm_back(grad_normed, gain_vector, unit_rows, inverse):
    scaled = grad_normed * gain_vector
    return inverse * (scaled - unit_rows * jnp.mean(scaled * unit_rows, axis=-1, keepdims=True))


def rotate(values):
    middle = values.shape[-1] // 2
    return jnp.concatenate([-values[..., middle:], values[..., :middle]], axis=-1)


def unrotate(values):
    middle = values.shape[-1] // 2
    return jnp.concatenate([values[..., middle:], -values[..., :middle]], axis=-1)


def split_pair(values):
    high = values.astype(BF16)
    rest = values - lax.reduce_precision(values, exponent_bits=8, mantissa_bits=7)
    return high, rest.astype(BF16)


def shifted(block, axis, step):
    count = lax.axis_size(axis)
    return lax.ppermute(block, axis, [(i, (i + step) % count) for i in range(count)])


def gather_blocks(block, axis):
    count = lax.axis_size(axis)
    return [block] + [shifted(block, axis, step) for step in range(1, count)]


def send_blocks(blocks, axis):
    return [shifted(blocks[step], axis, -step) for step in range(1, len(blocks))]


def split_rows(values, count):
    rows = values.shape[0] // count
    return [values[j * rows : (j + 1) * rows] for j in range(count)]


def add_up(values):
    total = values[0].astype(F32)
    for value in values[1:]:
        total = total + value.astype(F32)
    return total


def ordered_sum(values, axis):
    count = lax.axis_size(axis)
    place = lax.axis_index(axis)
    blocks = gather_blocks(values, axis)
    total = None
    for j in range(count):
        steps = (place - j) % count
        block = blocks[0]
        for step in range(1, count):
            block = jnp.where(steps == step, blocks[step], block)
        total = block if total is None else total + block
    return total


def swapped_or_none(values, axis):
    return swapped(values, axis, 1) if lax.axis_size(axis) == 2 else None


def whole_sum(values, other, axis):
    if other is not None:
        return values.astype(F32) + other.astype(F32)
    return lax.psum(values, axis).astype(F32)


def swapped(values, axis, bit):
    count = lax.axis_size(axis)
    return lax.ppermute(values, axis, [(i, i ^ bit) for i in range(count)])


def in_order(values, other, place, bit):
    first = (place & bit) == 0
    return jnp.concatenate(
        [jnp.where(first, values, other), jnp.where(first, other, values)], axis=0
    )


def after(value, *others):
    return lax.optimization_barrier((value,) + others)[0]


def move_blocks(moves, shapes, arrays, name):
    count = len(moves(0, 0, 0))

    def shape_of(move):
        index = move[1] if isinstance(move[1], tuple) else (move[1],)
        whole = arrays[move[0]].shape
        return tuple(i.size for i in index) + whole[len(index) :]

    def kernel(*refs):
        given, made = refs[: len(arrays)], refs[len(arrays) : len(arrays) + len(shapes)]
        held, (came, gone) = refs[len(arrays) + len(shapes) : -2], refs[-2:]
        todo = moves(lax.axis_index("dp"), lax.axis_index("ep"), lax.axis_index("tp"))
        loads = [
            pltpu.make_async_copy(given[move[0]].at[move[1]], held[k], came.at[k])
            for k, move in enumerate(todo)
        ]
        stores = [
            pltpu.make_async_copy(held[k], made[move[2]].at[move[3]], gone.at[k])
            for k, move in enumerate(todo)
        ]
        for load in loads:
            load.start()
        for load, store in zip(loads, stores):
            load.wait()
            store.start()
        for store in stores:
            store.wait()

    size = sum(2 * shape.size * shape.dtype.itemsize for shape in shapes)
    anywhere = pl.BlockSpec(memory_space=pl.ANY)
    return pl.pallas_call(
        kernel,
        in_specs=[anywhere] * len(arrays),
        out_specs=[anywhere] * len(shapes),
        out_shape=shapes,
        scratch_shapes=[pltpu.VMEM(shape_of(move), BF16) for move in moves(0, 0, 0)]
        + [pltpu.SemaphoreType.DMA((count,))] * 2,
        compiler_params=pltpu.CompilerParams(vmem_limit_bytes=24 << 20),
        cost_estimate=pl.CostEstimate(flops=0, bytes_accessed=size, transcendentals=0),
        name=name,
    )(*arrays)


def expert_kernel(
    half_count,
    expert_count,
    place_ref,
    rows_ref,
    upstream_ref,
    mask_ref,
    pick_ref,
    router_ref,
    first_ref,
    down_ref,
    *refs,
):
    *back_refs, grad_ref, gated_ref, gate_scratch, extra_scratch, back_scratch = refs[-7:]
    rows, width = rows_ref.shape
    segments = gate_scratch.shape[0]
    seg = down_ref.shape[0] // segments
    logits = dot_nt(rows_ref[...], router_ref[...])
    lane = lax.broadcasted_iota(jnp.int32, logits.shape, 1)
    routed = lane < expert_count
    top = jnp.max(jnp.where(routed, logits, -1e30), axis=1, keepdims=True)
    powers = jnp.where(routed, jnp.exp(jnp.where(routed, logits, top) - top), 0.0)
    probs = powers / jnp.sum(powers, axis=1, keepdims=True)
    switch = jax.nn.sigmoid(logits)
    gates = jnp.where(routed, probs, jnp.where(lane == expert_count, switch, 0.0))
    gates = gates * mask_ref[...].astype(F32)
    for j in range(segments):
        column = jnp.sum(gates * pick_ref[j : j + 1, :], axis=1, keepdims=True)
        gate_scratch[j] = jnp.broadcast_to(column, (rows, LANES))
    extra_scratch[...] = jnp.zeros_like(extra_scratch)
    back_scratch[...] = dot_nt(upstream_ref[...], down_ref[...])

    @pl.loop(0, segments)
    def _(j):
        low = pl.multiple_of(j * seg, LANES)
        first = pl.multiple_of(2 * j * seg, LANES)
        second = pl.multiple_of((2 * j + 1) * seg, LANES)
        gate = jnp.concatenate([gate_scratch[j]] * (seg // LANES), axis=1)
        pre = dot_nt(rows_ref[...], first_ref[pl.ds(first, 2 * seg), :])
        pre_gate, pre_up = pre[:, :seg], pre[:, seg:]
        back_lin = back_scratch[:, pl.ds(low, seg)]
        sigmoid = jax.nn.sigmoid(pre_gate)
        act = pre_gate * sigmoid
        hidden_low = (act * pre_up).astype(BF16).astype(F32)
        gated_ref[:, pl.ds(low, seg)] = (gate * hidden_low).astype(BF16)
        total = jnp.sum(hidden_low * back_lin, axis=1, keepdims=True)
        total_high = total.astype(BF16).astype(F32)
        extra_scratch[...] += total_high * pick_ref[pl.ds(j, 1), :]
        extra_scratch[...] += (total - total_high) * pick_ref[pl.ds(segments + j, 1), :]
        hidden_grad = gate * back_lin
        grad_ref[:, pl.ds(second, seg)] = (hidden_grad * act).astype(BF16)
        slope = sigmoid * (1.0 + pre_gate * (1.0 - sigmoid))
        grad_ref[:, pl.ds(first, seg)] = (hidden_grad * pre_up * slope).astype(BF16)

    count = rows // half_count
    place = place_ref[pl.num_programs(0)]

    def store(columns, values):
        for b in range(half_count):
            slot = lax.rem(place - b + half_count, half_count)
            start = pl.multiple_of(slot * count, count)
            part = values[b * count : (b + 1) * count].astype(BF16)
            for k, back_ref in enumerate(back_refs):

                @pl.when(pl.program_id(0) == k)
                def _(back_ref=back_ref, part=part, start=start):
                    back_ref[pl.ds(start, count), columns] = part


    step = width // 2

    @pl.loop(0, width // step)
    def _(n):
        columns = pl.ds(pl.multiple_of(n * step, step), step)
        store(columns, dot_nn(grad_ref[...], first_ref[:, columns]))

    store(pl.ds(width, LANES), extra_scratch[...])


def run_experts(
    groups, tp_index, tp_count, expert_count, rows, upstream, mask, picks, router, first, down, earlier
):
    span_rows, width = rows.shape
    steps = len(groups)
    hidden_all = down.shape[0]
    segments = picks.shape[0] // 2
    group_rows = mask.shape[0] // 4
    here = lambda k, place: (place[k], 0)
    fixed = lambda k, place: (0, 0)

    def whole(array):
        return pl.BlockSpec(array.shape, fixed, pipeline_mode=pl.Buffered(1))

    in_specs = [
        pl.BlockSpec((group_rows, width), here),
        pl.BlockSpec((group_rows, width), here),
        pl.BlockSpec((group_rows, LANES), here),
        whole(picks),
        whole(router),
        whole(first),
        whole(down),
    ] + [pl.BlockSpec(memory_space=pl.ANY)] * len(earlier)
    flops = 2 * steps * group_rows * width * 5 * hidden_all
    return pl.pallas_call(
        lambda *refs: expert_kernel(tp_count, expert_count, *refs),
        grid_spec=pltpu.PrefetchScalarGridSpec(
            num_scalar_prefetch=1,
            grid=(steps,),
            in_specs=in_specs,
            out_specs=[pl.BlockSpec((group_rows, width + LANES), fixed)] * 2
            + [
                pl.BlockSpec((group_rows, 2 * hidden_all), here),
                pl.BlockSpec((group_rows, hidden_all), here),
            ],
            scratch_shapes=[
                pltpu.VMEM((segments, group_rows, LANES), F32),
                pltpu.VMEM((group_rows, LANES), F32),
                pltpu.VMEM((group_rows, hidden_all), F32),
            ],
        ),
        out_shape=[jax.ShapeDtypeStruct((group_rows, width + LANES), BF16)] * 2
        + [
            jax.ShapeDtypeStruct((span_rows, 2 * hidden_all), BF16),
            jax.ShapeDtypeStruct((span_rows, hidden_all), BF16),
        ],
        input_output_aliases={8 + i: 2 + i for i in range(len(earlier))},
        compiler_params=pltpu.CompilerParams(vmem_limit_bytes=58 << 20),
        cost_estimate=pl.CostEstimate(
            flops=flops,
            bytes_accessed=2 * (first.size + down.size + steps * group_rows * (3 * width + 3 * hidden_all)),
            transcendentals=steps * group_rows * hidden_all,
        ),
        name="experts",
    )(jnp.stack([*groups, tp_index]).astype(jnp.int32), rows, upstream, mask, picks, router, first, down, *earlier)


def body(
    layer_input,
    cotangent,
    lengths,
    seq_order,
    routes,
    query_weight,
    key_weight,
    value_weight,
    mixing_weight,
    heads_bias,
    entry_gain,
    middle_gain,
    router_weight,
    shared_switch,
    shared_gate,
    shared_up,
    shared_down,
    expert_gate,
    expert_up,
    expert_down,
):
    tp_count = lax.axis_size("tp")
    ep_count = lax.axis_size("ep")
    dp_count = lax.axis_size("dp")
    part_count = dp_count * ep_count
    tp_index = lax.axis_index("tp")
    ep_index = lax.axis_index("ep")
    own_rows, width = layer_input.shape
    group_rows = own_rows * tp_count
    span_rows = group_rows * ep_count
    slice_rows = query_weight.shape[0]
    head_cols = query_weight.shape[1]
    head_count = head_cols // HD
    local_experts = expert_gate.shape[0]
    expert_count = router_weight.shape[1]
    hidden = expert_gate.shape[2]
    shared_hidden = shared_gate.shape[1] // ep_count
    segments = local_experts + 1
    seg = -(-max(hidden, shared_hidden) // LANES) * LANES

    span_lengths = jnp.take(
        lengths,
        lax.dynamic_slice_in_dim(seq_order, lax.axis_index("dp") * ep_count, ep_count, 0),
    )
    length = span_lengths[ep_index]
    own_keep = ((tp_index * own_rows + jnp.arange(own_rows)) < length).astype(F32)[:, None]
    block_of = jnp.arange(group_rows) // own_rows
    position = ((tp_index - block_of) % tp_count) * own_rows + jnp.arange(group_rows) % own_rows

    span_keep = (jnp.arange(group_rows)[None, :] < span_lengths[:, None]).reshape(span_rows, 1)
    lanes = jnp.arange(LANES)[None, :]
    column_of = jnp.concatenate(
        [ep_index * local_experts + jnp.arange(local_experts), jnp.array([expert_count])]
    )
    half = LANES // 2
    picks = jnp.concatenate([column_of, column_of + half])[:, None] == lanes
    picks = picks.astype(F32)

    bias_rows = heads_bias.size
    small = jnp.concatenate(
        [
            router_weight,
            shared_switch[:, None],
            entry_gain[:, None],
            middle_gain[:, None],
        ],
        axis=1,
    )
    bias_depth = -(-bias_rows // slice_rows)
    bias_cols = jnp.pad(heads_bias.reshape(-1), (0, bias_depth * slice_rows - bias_rows))
    bias_cols = bias_cols.reshape(bias_depth, slice_rows).T
    route_depth = -(-routes.size // slice_rows)
    route_cols = jnp.pad(routes.reshape(-1), (0, route_depth * slice_rows - routes.size))
    route_cols = route_cols.reshape(route_depth, slice_rows).T.astype(BF16)
    small = jnp.concatenate([small, bias_cols, route_cols], axis=1)
    small = jnp.pad(small, ((0, 0), (0, LANES - small.shape[1])))
    dense_own = jnp.concatenate(
        [query_weight, key_weight, value_weight, small], axis=1
    )
    dense_full = lax.all_gather(dense_own, ("dp", "ep"), axis=0, tiled=True)
    in_weight = dense_full[:, : 3 * head_cols]
    small_full = dense_full[:, 3 * head_cols :]
    out_weight = lax.all_gather(
        after(mixing_weight, dense_full), ("dp", "ep"), axis=1, tiled=True
    )
    small_rows = small_full[:, : expert_count + 3].astype(F32).T
    entry_full = small_rows[expert_count + 1][None]
    middle_full = small_rows[expert_count + 2][None]
    bias_full = small_full[:, expert_count + 3 : expert_count + 3 + bias_depth]
    bias_full = bias_full.reshape(part_count, slice_rows, bias_depth).transpose(0, 2, 1)
    bias_full = bias_full.reshape(part_count, -1)[:, :bias_rows]
    bias_full = bias_full.reshape((part_count,) + heads_bias.shape).transpose(1, 2, 0, 3)
    bias_full = bias_full.reshape(1, 3 * head_cols).astype(F32)

    route_at = expert_count + 3 + bias_depth
    span_routes = lax.dynamic_slice_in_dim(
        small_full[:, route_at : route_at + route_depth],
        lax.axis_index("dp") * ep_count * slice_rows,
        ep_count * slice_rows,
        0,
    )
    span_routes = span_routes.reshape(ep_count, slice_rows, route_depth).transpose(0, 2, 1)
    span_routes = span_routes.reshape(ep_count, -1)[:, : routes.size].reshape(span_rows, TOP)
    named = lanes == expert_count
    for k in range(TOP):
        named = named | (lanes == span_routes[:, k : k + 1].astype(jnp.int32))
    span_mask = (named & span_keep).astype(BF16)

    input_blocks = gather_blocks(layer_input, "tp")
    grad_blocks = gather_blocks(after(cotangent, input_blocks), "tp")
    input_values = jnp.concatenate(input_blocks, axis=0)

    def to_owners(matrix):
        return matrix.reshape(ep_count, shared_hidden, slice_rows)

    shared_own = jnp.concatenate(
        [to_owners(shared_gate.T), to_owners(shared_up.T), to_owners(shared_down)], axis=1
    )
    shared_own = after(shared_own, dense_full)
    shared_span = lax.all_to_all(shared_own, "ep", split_axis=0, concat_axis=0, tiled=True)
    freqs = THETA ** (-(jnp.arange(HD // 2).astype(F32) * 2.0) / HD)
    angles = position.astype(F32)[:, None] * freqs[None, :]
    angles = jnp.concatenate([angles, angles], axis=-1)
    cosine = jnp.cos(angles)[:, None, :]
    sine = jnp.sin(angles)[:, None, :]
    input_values = after(input_values, picks, cosine, sine).astype(F32)
    entry_unit, entry_inverse = norm_parts(input_values)
    entry_normed = (entry_unit * entry_full).astype(BF16)
    in_lin = dot_nn(entry_normed, in_weight) + bias_full
    query_heads = in_lin[:, :head_cols].reshape(group_rows, head_count, HD)
    key_heads = in_lin[:, head_cols : 2 * head_cols].reshape(group_rows, head_count, HD)
    query_rot = (query_heads * cosine + rotate(query_heads) * sine).astype(BF16)
    key_rot = (key_heads * cosine + rotate(key_heads) * sine).astype(BF16)
    value_heads = in_lin[:, 2 * head_cols :].astype(BF16).reshape(group_rows, head_count, HD)
    score_scale = HD ** (-0.5)
    causal = position[:, None] >= position[None, :]

    def score_matrix():
        raw_scores = jnp.einsum("qhd,khd->hqk", query_rot, key_rot, preferred_element_type=F32)
        return jnp.where(causal[None], raw_scores * score_scale, -1e30)

    scores = score_matrix()
    top_score = jnp.max(scores, axis=-1, keepdims=True)
    log_total = top_score + jnp.log(jnp.sum(jnp.exp(scores - top_score), axis=-1, keepdims=True))
    attn_probs = jnp.exp(scores - log_total).astype(BF16)
    context = jnp.einsum("hqk,khd->qhd", attn_probs, value_heads, preferred_element_type=F32)
    context_low = context.astype(BF16).reshape(group_rows, head_cols)
    context_low = after(context_low, shared_span)
    head_blocks = split_rows(dot_nn(context_low, out_weight).astype(BF16), tp_count)
    attention_parts = send_blocks(head_blocks, "tp")

    shared_span = after(shared_span, head_blocks)
    if dp_count == 2:
        shared_other = swapped(shared_span, "dp", 1)
        attention_parts = after(attention_parts, shared_other)
        shared_parts = in_order(shared_span, shared_other, lax.axis_index("dp"), 1)
    else:
        shared_parts = lax.all_gather(shared_span, "dp", axis=0, tiled=True)
    shared_parts = shared_parts.reshape(part_count, 3, shared_hidden, slice_rows)
    shared_parts = shared_parts.transpose(1, 2, 0, 3).reshape(3, shared_hidden, width)

    def stack_hidden(expert_rows, shared_rows):
        padded = [jnp.pad(rows, ((0, seg - rows.shape[0]), (0, 0))) for rows in expert_rows]
        padded.append(jnp.pad(shared_rows, ((0, seg - shared_hidden), (0, 0))))
        return padded

    gate_rows = stack_hidden([expert_gate[j].T for j in range(local_experts)], shared_parts[0])
    up_rows = stack_hidden([expert_up[j].T for j in range(local_experts)], shared_parts[1])
    down_rows = stack_hidden([expert_down[j] for j in range(local_experts)], shared_parts[2])
    first_weight = jnp.concatenate(
        [rows for pair in zip(gate_rows, up_rows) for rows in pair], axis=0
    )
    down_weight = jnp.concatenate(down_rows, axis=0)

    grad_blocks = after(grad_blocks, head_blocks)
    group_upstream = jnp.concatenate(grad_blocks, axis=0)
    near = swapped(group_upstream, "ep", 2)

    attention_parts = after(attention_parts, near)
    attention_own = add_up([head_blocks[0], *attention_parts])
    hidden_state = input_values[:own_rows] + own_keep * attention_own
    middle_unit, middle_inverse = norm_parts(hidden_state)
    middle_normed = (middle_unit * middle_full).astype(BF16)

    span_normed = lax.all_gather(middle_normed, ("ep", "tp"), axis=0, tiled=True)
    sibling, far = swapped(group_upstream, "ep", 1), swapped(near, "ep", 1)

    def upstream_moves(_, place, turn):
        moves = []
        for k in range(4):
            for j in range(tp_count):
                block = (place ^ k) * tp_count + lax.rem(turn - j + tp_count, tp_count)
                start = pl.multiple_of(block * own_rows, own_rows)
                moves.append((k, pl.ds(j * own_rows, own_rows), 0, pl.ds(start, own_rows)))
        return moves

    upstream = move_blocks(
        upstream_moves,
        [jax.ShapeDtypeStruct((span_rows, width), BF16)],
        [group_upstream, sibling, near, far],
        "order_rows",
    )[0]

    own_logits = dot_nn(middle_normed, small_full)
    expert_probs = jax.nn.softmax(own_logits[:, :expert_count], axis=-1)
    switch_value = jax.nn.sigmoid(own_logits[:, expert_count : expert_count + 1])
    own_routes = lax.dynamic_slice_in_dim(routes, tp_index * own_rows, own_rows, 0)
    route_mask = jnp.any(
        own_routes[:, :, None] == jnp.arange(expert_count)[None, None, :], axis=1
    ).astype(F32)

    first_weight, down_weight = after((first_weight, down_weight), middle_normed)
    span_mask = after(span_mask, expert_probs, switch_value, route_mask)
    shared_operands = (span_normed, upstream, span_mask, picks, small_full.T, first_weight, down_weight)
    sibling_back, chip_back, *made = run_experts(
        (ep_index ^ 3, ep_index ^ 2), tp_index, tp_count, expert_count, *shared_operands, ()
    )
    chip_sum = add_up([chip_back, swapped(sibling_back, "ep", 1)]).astype(BF16)
    from_chip = swapped(chip_sum, "ep", 2)
    sibling_back, group_back, first_grad, hidden_gated = run_experts(
        (after(ep_index ^ 1, chip_sum), ep_index),
        tp_index,
        tp_count,
        expert_count,
        *shared_operands,
        made,
    )
    from_core = [swapped(block, "ep", 1) for block in split_rows(sibling_back, tp_count)]
    down_grad = dot_tn(hidden_gated, upstream).astype(BF16)

    def last_moves(*_):
        return [
            (0, pl.ds(j * seg, hidden), 0, pl.ds(j * hidden, hidden)) for j in range(local_experts)
        ]

    last_own = move_blocks(
        last_moves,
        [jax.ShapeDtypeStruct((local_experts * hidden, width), BF16)],
        [down_grad],
        "down_rows",
    )[0]
    last_other = swapped_or_none(last_own, "dp")
    from_core = after(from_core, last_own)
    back_blocks = [
        add_up(blocks)
        for blocks in zip(
            split_rows(group_back, tp_count), from_core, split_rows(from_chip, tp_count)
        )
    ]
    back_blocks = [back_blocks[0]] + [block.astype(BF16) for block in back_blocks[1:]]
    back_parts = send_blocks(back_blocks, "tp")

    first_grad = after(first_grad, back_blocks)
    first_weight_grad = dot_tn(first_grad, span_normed).astype(BF16)
    shared_size = width // dp_count

    def first_moves(place, *_):
        moves = [
            (0, pl.ds((2 * j + part) * seg, hidden), part, pl.ds(j * hidden, hidden))
            for part in range(2)
            for j in range(local_experts)
        ]
        starts = (place, 1 - place) if dp_count == 2 else (0, 0)
        for k, start in enumerate(starts):
            columns = pl.ds(0, width)
            if dp_count == 2:
                columns = pl.ds(pl.multiple_of(start * shared_size, LANES), shared_size)
            for part, (array, base) in enumerate(
                ((0, 2 * local_experts * seg), (0, (2 * local_experts + 1) * seg), (1, local_experts * seg))
            ):
                moves.append(
                    (
                        array,
                        (pl.ds(base, shared_hidden), columns),
                        2 + k,
                        pl.ds(part * shared_hidden, shared_hidden),
                    )
                )
        return moves

    shared_shape = (3 * shared_hidden, shared_size if dp_count == 2 else width)
    *first_own, shared_kept, shared_given = move_blocks(
        first_moves,
        [jax.ShapeDtypeStruct((local_experts * hidden, width), BF16)] * 2
        + [jax.ShapeDtypeStruct(shared_shape, BF16)] * 2,
        [first_weight_grad, down_grad],
        "first_rows",
    )
    first_other = [swapped_or_none(part, "dp") for part in first_own]
    hidden_gated = after(hidden_gated, first_own)
    branch = dot_nn(hidden_gated, down_weight).astype(BF16)
    branch_terms = lax.all_to_all(
        branch.reshape(ep_count, group_rows, width), "ep", split_axis=0, concat_axis=0, tiled=True
    )
    back_parts = after(back_parts, branch, shared_kept, shared_given)
    if dp_count == 2:
        back_parts = after(back_parts, last_other)
    back_own = add_up([back_blocks[0], *back_parts])

    normed_own = back_own[:, :width]
    gate_sums = back_own[:, width : width + half] + back_own[:, width + half :]
    prob_grad = own_keep * route_mask * gate_sums[:, :expert_count]
    logit_grad = expert_probs * (
        prob_grad - jnp.sum(expert_probs * prob_grad, axis=-1, keepdims=True)
    )
    switch_grad = (
        own_keep
        * gate_sums[:, expert_count : expert_count + 1]
        * switch_value
        * (1.0 - switch_value)
    )
    score_grad = jnp.concatenate([logit_grad, switch_grad], axis=1)
    normed_total = normed_own + dot_exact(score_grad, small_rows[: expert_count + 1], ((1,), (0,)))
    router_part = dot_exact(score_grad, middle_normed.astype(F32), ((0,), (0,)))
    middle_part = jnp.sum(normed_total * middle_unit, axis=0, keepdims=True)
    state_grad = cotangent.astype(F32) + norm_back(
        normed_total, middle_full, middle_unit, middle_inverse
    )
    attention_grad_own = (own_keep * state_grad).astype(BF16)
    attention_grad_blocks = gather_blocks(attention_grad_own, "tp")

    if dp_count == 2:
        attention_grad_blocks = after(attention_grad_blocks, first_other[0])
    attention_grad = jnp.concatenate(attention_grad_blocks, axis=0)
    shared_other = swapped_or_none(shared_given, "dp")

    mixing_grad = dot_tn(attention_grad, context_low).astype(BF16)
    context_grad = dot_nt(attention_grad, out_weight)
    context_grad = context_grad.astype(BF16).reshape(group_rows, head_count, HD)
    probs_again = jnp.exp(score_matrix() - log_total)
    probs_low = probs_again.astype(BF16)
    value_grad = jnp.einsum("hqk,qhd->khd", probs_low, context_grad, preferred_element_type=F32)
    value_grad = value_grad.astype(BF16).reshape(group_rows, head_cols)
    prob_grads = jnp.einsum("qhd,khd->hqk", context_grad, value_heads, preferred_element_type=F32)
    row_delta = jnp.sum(probs_again * prob_grads, axis=-1, keepdims=True)
    score_grads = (probs_again * (prob_grads - row_delta)).astype(BF16)
    query_rot_grad = (
        jnp.einsum("hqk,khd->qhd", score_grads, key_rot, preferred_element_type=F32) * score_scale
    )
    key_rot_grad = (
        jnp.einsum("hqk,qhd->khd", score_grads, query_rot, preferred_element_type=F32) * score_scale
    )
    query_grad = (query_rot_grad * cosine + unrotate(query_rot_grad * sine)).astype(BF16)
    key_grad = (key_rot_grad * cosine + unrotate(key_rot_grad * sine)).astype(BF16)
    in_grad = jnp.concatenate(
        [query_grad.reshape(group_rows, head_cols), key_grad.reshape(group_rows, head_cols), value_grad],
        axis=1,
    )
    bias_grad = jnp.sum(in_grad.astype(F32), axis=0)
    entry_part = dot_nt(in_grad, in_weight)
    entry_blocks = split_rows(entry_part.astype(BF16), tp_count)
    entry_parts = send_blocks(entry_blocks, "tp")
    if dp_count == 2:
        shared_mine = add_up([shared_kept, after(shared_other, entry_parts)]).astype(BF16)
    else:
        shared_mine = lax.psum_scatter(shared_kept, "dp", scatter_dimension=1, tiled=True)
    shared_mine = shared_mine.reshape(3 * shared_hidden, ep_count, slice_rows).transpose(1, 0, 2)
    shared_back = lax.all_to_all(shared_mine, "ep", split_axis=0, concat_axis=0, tiled=True)
    shared_back = shared_back.reshape(ep_count, 3, shared_hidden, slice_rows).astype(F32)
    entry_own = add_up([entry_blocks[0], *entry_parts])
    input_gradient = state_grad + norm_back(
        entry_own, entry_full, entry_unit[:own_rows], entry_inverse[:own_rows]
    )

    entry_gain_part = jnp.sum(entry_part * entry_unit, axis=0, keepdims=True)
    small_part = jnp.concatenate([router_part, middle_part, entry_gain_part], axis=0)
    bias_part = bias_grad.reshape(3, head_count, part_count, -1).transpose(2, 0, 1, 3)
    bias_part = bias_part.reshape(part_count, bias_rows)
    bias_part = jnp.pad(bias_part, ((0, 0), (0, bias_depth * slice_rows - bias_rows)))
    bias_part = bias_part.reshape(part_count, bias_depth, slice_rows).transpose(1, 0, 2)
    bias_part = bias_part.reshape(bias_depth, width)
    small_part = jnp.concatenate([small_part, bias_part], axis=0)
    small_high, small_low = split_pair(small_part)
    small_count = small_part.shape[0]
    small_cols = jnp.concatenate(
        [
            jnp.pad(small_high, ((0, half - small_count), (0, 0))),
            jnp.pad(small_low, ((0, half - small_count), (0, 0))),
        ],
        axis=0,
    ).T
    dense_grad = jnp.concatenate(
        [
            dot_tn(entry_normed, in_grad).astype(BF16),
            mixing_grad,
            small_cols,
        ],
        axis=1,
    )
    if dp_count == 2:
        dense_grad = after(dense_grad, first_other[1], branch_terms)
    dense_sum = lax.psum_scatter(
        dense_grad, ("dp", "ep"), scatter_dimension=0, tiled=True
    ).astype(F32)
    small_sum = dense_sum[:, 4 * head_cols : 4 * head_cols + half] + dense_sum[:, 4 * head_cols + half :]
    tp_sum = ordered_sum(small_sum[:, : expert_count + 3].T, "tp")
    bias_sum = small_sum[:, expert_count + 3 : expert_count + 3 + bias_depth]
    bias_sum = bias_sum.T.reshape(-1)[:bias_rows].reshape(heads_bias.shape)

    branch_terms = after(branch_terms, entry_blocks)
    branch_blocks = []
    for j in range(tp_count):
        start = ((tp_index - j) % tp_count) * own_rows
        rows = lax.dynamic_slice_in_dim(branch_terms, start, own_rows, 1)
        branch_blocks.append(jnp.sum(rows.astype(F32), axis=0))
    branch_blocks = [branch_blocks[0]] + [block.astype(BF16) for block in branch_blocks[1:]]
    branch_parts = send_blocks(branch_blocks, "tp")
    layer_output = (hidden_state + add_up([branch_blocks[0], *branch_parts])).astype(BF16)
    if dp_count == 2:
        first_other = after(first_other, entry_parts, tp_sum)
    first_sum = [
        whole_sum(own, other, "dp").reshape(local_experts, hidden, width)
        for own, other in zip(first_own, first_other)
    ]
    last_sum = whole_sum(last_own, last_other, "dp").reshape(local_experts, hidden, width)

    def by_columns(rows):
        return rows.transpose(2, 0, 1).reshape(slice_rows, ep_count * shared_hidden)

    return (
        layer_output,
        input_gradient,
        dense_sum[:, :head_cols],
        dense_sum[:, head_cols : 2 * head_cols],
        dense_sum[:, 2 * head_cols : 3 * head_cols],
        dense_sum[:, 3 * head_cols : 4 * head_cols].T,
        bias_sum,
        tp_sum[expert_count + 2],
        tp_sum[expert_count + 1],
        tp_sum[:expert_count].T,
        tp_sum[expert_count],
        by_columns(shared_back[:, 0]),
        by_columns(shared_back[:, 1]),
        shared_back[:, 2].reshape(ep_count * shared_hidden, slice_rows),
        first_sum[0].transpose(0, 2, 1),
        first_sum[1].transpose(0, 2, 1),
        last_sum,
    )


def solution(mesh):
    rows = P(("dp", "ep", "tp"), None)
    parts = P(("dp", "ep"))
    in_cols = P(("dp", "ep"), "tp")
    out_cols = P("tp", ("dp", "ep"))
    weights = (
        in_cols,
        in_cols,
        in_cols,
        out_cols,
        P(None, "tp", ("dp", "ep")),
        parts,
        parts,
        P(("dp", "ep"), None),
        parts,
        in_cols,
        in_cols,
        out_cols,
        P("ep", None, "tp"),
        P("ep", None, "tp"),
        P("ep", "tp", None),
    )
    return jax.shard_map(
        body,
        mesh=mesh,
        in_specs=(rows, rows, P(), P(), P(("dp", "ep"), None)) + weights,
        out_specs=(rows, rows) + weights,
        check_vma=False,
    )
```

```python
import jax
import jax.numpy as jnp
from jax import lax
from jax.experimental import pallas as pl
from jax.experimental.pallas import tpu as pltpu
from jax.sharding import PartitionSpec as P

HD = 128
TOP = 4
EPS = 1e-06
THETA = 1000000.0
LANES = 128
F32 = jnp.float32
BF16 = jnp.bfloat16


def dot_nn(left, right):
    return lax.dot_general(left, right, (((1,), (0,)), ((), ())), preferred_element_type=F32)


def dot_nt(left, right):
    return lax.dot_general(left, right, (((1,), (1,)), ((), ())), preferred_element_type=F32)


def dot_tn(left, right):
    return lax.dot_general(left, right, (((0,), (0,)), ((), ())), preferred_element_type=F32)


def norm_parts(values):
    inverse = lax.rsqrt(jnp.mean(values * values, axis=-1, keepdims=True) + EPS)
    return (values * inverse, inverse)


def norm_back(grad_normed, gain_vector, unit_rows, inverse):
    scaled = grad_normed * gain_vector
    return inverse * (scaled - unit_rows * jnp.mean(scaled * unit_rows, axis=-1, keepdims=True))


def rotate(values):
    middle = values.shape[-1] // 2
    return jnp.concatenate([-values[..., middle:], values[..., :middle]], axis=-1)


def unrotate(values):
    middle = values.shape[-1] // 2
    return jnp.concatenate([values[..., middle:], -values[..., :middle]], axis=-1)


def split_pair(values):
    high = values.astype(BF16)
    rest = values - lax.reduce_precision(values, exponent_bits=8, mantissa_bits=7)
    return high, rest.astype(BF16)


def shifted(block, axis, step):
    count = lax.axis_size(axis)
    return lax.ppermute(block, axis, [(i, (i + step) % count) for i in range(count)])


def gather_blocks(block, axis):
    count = lax.axis_size(axis)
    return [block] + [shifted(block, axis, step) for step in range(1, count)]


def send_blocks(blocks, axis):
    return [shifted(blocks[step], axis, -step) for step in range(1, len(blocks))]


def split_rows(values, count):
    rows = values.shape[0] // count
    return [values[j * rows : (j + 1) * rows] for j in range(count)]


def add_up(values):
    total = values[0].astype(F32)
    for value in values[1:]:
        total = total + value.astype(F32)
    return total


def ordered_sum(values, axis, beside):
    count = lax.axis_size(axis)
    place = lax.axis_index(axis)
    blocks = after(gather_blocks(values, axis), beside)
    total = None
    for j in range(count):
        steps = (place - j) % count
        block = blocks[0]
        for step in range(1, count):
            block = jnp.where(steps == step, blocks[step], block)
        total = block if total is None else total + block
    return total


def swapped_or_none(values, axis):
    return swapped(values, axis, 1) if lax.axis_size(axis) == 2 else None


def whole_sum(values, other, axis):
    if other is not None:
        return values.astype(F32) + other.astype(F32)
    return lax.psum(values, axis).astype(F32)


def swapped(values, axis, bit):
    count = lax.axis_size(axis)
    return lax.ppermute(values, axis, [(i, i ^ bit) for i in range(count)])


def in_order(values, other, place, bit):
    first = (place & bit) == 0
    return jnp.concatenate(
        [jnp.where(first, values, other), jnp.where(first, other, values)], axis=0
    )


def after(value, *others):
    return lax.optimization_barrier((value,) + others)[0]


def move_blocks(moves, shapes, arrays, name):
    count = len(moves(0, 0, 0))

    def shape_of(move):
        index = move[1] if isinstance(move[1], tuple) else (move[1],)
        whole = arrays[move[0]].shape
        return tuple(i.size for i in index) + whole[len(index) :]

    def kernel(*refs):
        given, made = refs[: len(arrays)], refs[len(arrays) : len(arrays) + len(shapes)]
        held, (came, gone) = refs[len(arrays) + len(shapes) : -2], refs[-2:]
        todo = moves(lax.axis_index("dp"), lax.axis_index("ep"), lax.axis_index("tp"))
        loads = [
            pltpu.make_async_copy(given[move[0]].at[move[1]], held[k], came.at[k])
            for k, move in enumerate(todo)
        ]
        stores = [
            pltpu.make_async_copy(held[k], made[move[2]].at[move[3]], gone.at[k])
            for k, move in enumerate(todo)
        ]
        for load in loads:
            load.start()
        for load, store in zip(loads, stores):
            load.wait()
            store.start()
        for store in stores:
            store.wait()

    size = sum(2 * shape.size * shape.dtype.itemsize for shape in shapes)
    anywhere = pl.BlockSpec(memory_space=pl.ANY)
    return pl.pallas_call(
        kernel,
        in_specs=[anywhere] * len(arrays),
        out_specs=[anywhere] * len(shapes),
        out_shape=shapes,
        scratch_shapes=[pltpu.VMEM(shape_of(move), BF16) for move in moves(0, 0, 0)]
        + [pltpu.SemaphoreType.DMA((count,))] * 2,
        compiler_params=pltpu.CompilerParams(vmem_limit_bytes=24 << 20),
        cost_estimate=pl.CostEstimate(flops=0, bytes_accessed=size, transcendentals=0),
        name=name,
    )(*arrays)


def expert_kernel(
    half_count,
    expert_count,
    place_ref,
    rows_ref,
    upstream_ref,
    mask_ref,
    pick_ref,
    router_ref,
    first_ref,
    down_ref,
    *refs,
):
    *back_refs, grad_ref, gated_ref, gate_scratch, extra_scratch, back_scratch = refs[-7:]
    rows, width = rows_ref.shape
    segments = gate_scratch.shape[0]
    seg = down_ref.shape[0] // segments
    logits = dot_nt(rows_ref[...], router_ref[...])
    lane = lax.broadcasted_iota(jnp.int32, logits.shape, 1)
    routed = lane < expert_count
    top = jnp.max(jnp.where(routed, logits, -1e30), axis=1, keepdims=True)
    powers = jnp.where(routed, jnp.exp(jnp.where(routed, logits, top) - top), 0.0)
    probs = powers / jnp.sum(powers, axis=1, keepdims=True)
    switch = jax.nn.sigmoid(logits)
    gates = jnp.where(routed, probs, jnp.where(lane == expert_count, switch, 0.0))
    gates = gates * mask_ref[...].astype(F32)
    for j in range(segments):
        column = jnp.sum(gates * pick_ref[j : j + 1, :], axis=1, keepdims=True)
        gate_scratch[j] = jnp.broadcast_to(column, (rows, LANES))
    extra_scratch[...] = jnp.zeros_like(extra_scratch)
    back_scratch[...] = dot_nt(upstream_ref[...], down_ref[...])

    @pl.loop(0, segments)
    def _(j):
        low = pl.multiple_of(j * seg, LANES)
        first = pl.multiple_of(2 * j * seg, LANES)
        second = pl.multiple_of((2 * j + 1) * seg, LANES)
        gate = jnp.concatenate([gate_scratch[j]] * (seg // LANES), axis=1)
        pre = dot_nt(rows_ref[...], first_ref[pl.ds(first, 2 * seg), :])
        pre_gate, pre_up = pre[:, :seg], pre[:, seg:]
        back_lin = back_scratch[:, pl.ds(low, seg)]
        sigmoid = jax.nn.sigmoid(pre_gate)
        act = pre_gate * sigmoid
        hidden_low = (act * pre_up).astype(BF16).astype(F32)
        gated_ref[:, pl.ds(low, seg)] = (gate * hidden_low).astype(BF16)
        total = jnp.sum(hidden_low * back_lin, axis=1, keepdims=True)
        total_high = total.astype(BF16).astype(F32)
        extra_scratch[...] += total_high * pick_ref[pl.ds(j, 1), :]
        extra_scratch[...] += (total - total_high) * pick_ref[pl.ds(segments + j, 1), :]
        hidden_grad = gate * back_lin
        grad_ref[:, pl.ds(second, seg)] = (hidden_grad * act).astype(BF16)
        slope = sigmoid * (1.0 + pre_gate * (1.0 - sigmoid))
        grad_ref[:, pl.ds(first, seg)] = (hidden_grad * pre_up * slope).astype(BF16)

    count = rows // half_count
    place = place_ref[pl.num_programs(0)]

    def store(columns, values):
        for b in range(half_count):
            slot = lax.rem(place - b + half_count, half_count)
            start = pl.multiple_of(slot * count, count)
            part = values[b * count : (b + 1) * count].astype(BF16)
            for k, back_ref in enumerate(back_refs):

                @pl.when(pl.program_id(0) == k)
                def _(back_ref=back_ref, part=part, start=start):
                    back_ref[pl.ds(start, count), columns] = part


    step = width // 2

    @pl.loop(0, width // step)
    def _(n):
        columns = pl.ds(pl.multiple_of(n * step, step), step)
        store(columns, dot_nn(grad_ref[...], first_ref[:, columns]))

    store(pl.ds(width, LANES), extra_scratch[...])


def own_kernel(expert_count, *refs):
    (first_ref, *part_refs) = refs[:-14]
    (
        probs_ref, mask_ref, switch_ref, keep_ref, small_ref, unit_ref, inverse_ref, normed_ref,
        upstream_ref, state_ref, low_ref, router_ref, middle_ref, total_ref,
    ) = refs[-14:]
    width = unit_ref.shape[1]
    total_ref[...] = first_ref[...]
    for part_ref in part_refs:
        total_ref[...] += part_ref[...].astype(F32)
    sums = total_ref[:, width:]
    sums = sums + pltpu.roll(sums, LANES // 2, axis=1)
    probs, mask = probs_ref[...], mask_ref[...]
    keep, switch = keep_ref[:, :1], switch_ref[:, :1]
    lane = lax.broadcasted_iota(jnp.int32, sums.shape, 1)
    prob_grad = jnp.where(lane < expert_count, keep * mask * sums, 0.0)
    mean = jnp.sum(probs * prob_grad, axis=1, keepdims=True)
    score = jnp.where(lane < expert_count, probs * (prob_grad - mean), 0.0)
    score = jnp.where(lane == expert_count, keep * sums * switch * (1.0 - switch), score)
    high = score.astype(BF16)
    low = (score - high.astype(F32)).astype(BF16)
    small = small_ref[...]
    normed_total = total_ref[:, :width] + dot_nn(high, small) + dot_nn(low, small)
    normed = normed_ref[...]
    router_ref[...] = dot_tn(high, normed) + dot_tn(low, normed)
    unit = unit_ref[...]
    middle_ref[...] = jnp.sum(normed_total * unit, axis=0, keepdims=True)
    gain = small[expert_count + 2 : expert_count + 3, :].astype(F32)
    state = upstream_ref[...].astype(F32) + norm_back(normed_total, gain, unit, inverse_ref[:, :1])
    state_ref[...] = state
    low_ref[...] = (keep * state).astype(BF16)


def run_own(expert_count, blocks, scores, small, unit, inverse, normed, upstream):
    rows, width = unit.shape
    wide = lambda column: jnp.broadcast_to(column, (rows, LANES))
    probs, mask, switch, keep = scores
    pad = lambda values: jnp.pad(values, ((0, 0), (0, LANES - values.shape[1])))
    operands = [
        *blocks, pad(probs), pad(mask), wide(switch), wide(keep), small, unit, wide(inverse), normed, upstream,
    ]
    return pl.pallas_call(
        lambda *refs: own_kernel(expert_count, *refs),
        in_specs=[pl.BlockSpec(memory_space=pltpu.VMEM)] * len(operands),
        out_specs=[pl.BlockSpec(memory_space=pltpu.VMEM)] * 4,
        out_shape=[
            jax.ShapeDtypeStruct((rows, width), F32),
            jax.ShapeDtypeStruct((rows, width), BF16),
            jax.ShapeDtypeStruct((LANES, width), F32),
            jax.ShapeDtypeStruct((1, width), F32),
        ],
        scratch_shapes=[pltpu.VMEM((rows, width + LANES), F32)],
        compiler_params=pltpu.CompilerParams(vmem_limit_bytes=24 << 20),
        cost_estimate=pl.CostEstimate(
            flops=60 * 8 * rows * width * LANES, bytes_accessed=24 * rows * width, transcendentals=0
        ),
        name="own_rows",
    )(*operands)


def run_experts(
    groups, tp_index, tp_count, expert_count, rows, upstream, mask, picks, router, first, down, earlier
):
    span_rows, width = rows.shape
    steps = len(groups)
    hidden_all = down.shape[0]
    segments = picks.shape[0] // 2
    group_rows = mask.shape[0] // 4
    here = lambda k, place: (place[k], 0)
    fixed = lambda k, place: (0, 0)

    def whole(array):
        return pl.BlockSpec(array.shape, fixed, pipeline_mode=pl.Buffered(1))

    in_specs = [
        pl.BlockSpec((group_rows, width), here),
        pl.BlockSpec((group_rows, width), here),
        pl.BlockSpec((group_rows, LANES), here),
        whole(picks),
        whole(router),
        whole(first),
        whole(down),
    ] + [pl.BlockSpec(memory_space=pl.ANY)] * len(earlier)
    flops = 2 * steps * group_rows * width * 5 * hidden_all
    return pl.pallas_call(
        lambda *refs: expert_kernel(tp_count, expert_count, *refs),
        grid_spec=pltpu.PrefetchScalarGridSpec(
            num_scalar_prefetch=1,
            grid=(steps,),
            in_specs=in_specs,
            out_specs=[pl.BlockSpec((group_rows, width + LANES), fixed)] * 2
            + [
                pl.BlockSpec((group_rows, 2 * hidden_all), here),
                pl.BlockSpec((group_rows, hidden_all), here),
            ],
            scratch_shapes=[
                pltpu.VMEM((segments, group_rows, LANES), F32),
                pltpu.VMEM((group_rows, LANES), F32),
                pltpu.VMEM((group_rows, hidden_all), F32),
            ],
        ),
        out_shape=[jax.ShapeDtypeStruct((group_rows, width + LANES), BF16)] * 2
        + [
            jax.ShapeDtypeStruct((span_rows, 2 * hidden_all), BF16),
            jax.ShapeDtypeStruct((span_rows, hidden_all), BF16),
        ],
        input_output_aliases={8 + i: 2 + i for i in range(len(earlier))},
        compiler_params=pltpu.CompilerParams(vmem_limit_bytes=58 << 20),
        cost_estimate=pl.CostEstimate(
            flops=flops,
            bytes_accessed=2 * (first.size + down.size + steps * group_rows * (3 * width + 3 * hidden_all)),
            transcendentals=steps * group_rows * hidden_all,
        ),
        name="experts",
    )(jnp.stack([*groups, tp_index]).astype(jnp.int32), rows, upstream, mask, picks, router, first, down, *earlier)


def body(
    layer_input,
    cotangent,
    lengths,
    seq_order,
    routes,
    query_weight,
    key_weight,
    value_weight,
    mixing_weight,
    heads_bias,
    entry_gain,
    middle_gain,
    router_weight,
    shared_switch,
    shared_gate,
    shared_up,
    shared_down,
    expert_gate,
    expert_up,
    expert_down,
):
    tp_count = lax.axis_size("tp")
    ep_count = lax.axis_size("ep")
    dp_count = lax.axis_size("dp")
    part_count = dp_count * ep_count
    tp_index = lax.axis_index("tp")
    ep_index = lax.axis_index("ep")
    own_rows, width = layer_input.shape
    group_rows = own_rows * tp_count
    span_rows = group_rows * ep_count
    slice_rows = query_weight.shape[0]
    head_cols = query_weight.shape[1]
    head_count = head_cols // HD
    local_experts = expert_gate.shape[0]
    expert_count = router_weight.shape[1]
    hidden = expert_gate.shape[2]
    shared_hidden = shared_gate.shape[1] // ep_count
    segments = local_experts + 1
    seg = -(-max(hidden, shared_hidden) // LANES) * LANES

    span_lengths = jnp.take(
        lengths,
        lax.dynamic_slice_in_dim(seq_order, lax.axis_index("dp") * ep_count, ep_count, 0),
    )
    length = span_lengths[ep_index]
    own_keep = ((tp_index * own_rows + jnp.arange(own_rows)) < length).astype(F32)[:, None]
    block_of = jnp.arange(group_rows) // own_rows
    position = ((tp_index - block_of) % tp_count) * own_rows + jnp.arange(group_rows) % own_rows

    span_keep = (jnp.arange(group_rows)[None, :] < span_lengths[:, None]).reshape(span_rows, 1)
    lanes = jnp.arange(LANES)[None, :]
    column_of = jnp.concatenate(
        [ep_index * local_experts + jnp.arange(local_experts), jnp.array([expert_count])]
    )
    half = LANES // 2
    picks = jnp.concatenate([column_of, column_of + half])[:, None] == lanes
    picks = picks.astype(F32)

    bias_rows = heads_bias.size
    small = jnp.concatenate(
        [
            router_weight,
            shared_switch[:, None],
            entry_gain[:, None],
            middle_gain[:, None],
        ],
        axis=1,
    )
    bias_depth = -(-bias_rows // slice_rows)
    bias_cols = jnp.pad(heads_bias.reshape(-1), (0, bias_depth * slice_rows - bias_rows))
    bias_cols = bias_cols.reshape(bias_depth, slice_rows).T
    route_depth = -(-routes.size // slice_rows)
    route_cols = jnp.pad(routes.reshape(-1), (0, route_depth * slice_rows - routes.size))
    route_cols = route_cols.reshape(route_depth, slice_rows).T.astype(BF16)
    small = jnp.concatenate([small, bias_cols, route_cols], axis=1)
    small = jnp.pad(small, ((0, 0), (0, LANES - small.shape[1])))
    dense_own = jnp.concatenate(
        [query_weight, key_weight, value_weight, small], axis=1
    )
    dense_full = lax.all_gather(dense_own, ("dp", "ep"), axis=0, tiled=True)
    in_weight = dense_full[:, : 3 * head_cols]
    small_full = dense_full[:, 3 * head_cols :]
    out_weight = lax.all_gather(
        after(mixing_weight, dense_full), ("dp", "ep"), axis=1, tiled=True
    )
    small_rows = small_full[:, : expert_count + 3].astype(F32).T
    entry_full = small_rows[expert_count + 1][None]
    middle_full = small_rows[expert_count + 2][None]
    bias_full = small_full[:, expert_count + 3 : expert_count + 3 + bias_depth]
    bias_full = bias_full.reshape(part_count, slice_rows, bias_depth).transpose(0, 2, 1)
    bias_full = bias_full.reshape(part_count, -1)[:, :bias_rows]
    bias_full = bias_full.reshape((part_count,) + heads_bias.shape).transpose(1, 2, 0, 3)
    bias_full = bias_full.reshape(1, 3 * head_cols).astype(F32)

    route_at = expert_count + 3 + bias_depth
    span_routes = lax.dynamic_slice_in_dim(
        small_full[:, route_at : route_at + route_depth],
        lax.axis_index("dp") * ep_count * slice_rows,
        ep_count * slice_rows,
        0,
    )
    span_routes = span_routes.reshape(ep_count, slice_rows, route_depth).transpose(0, 2, 1)
    span_routes = span_routes.reshape(ep_count, -1)[:, : routes.size].reshape(span_rows, TOP)
    named = lanes == expert_count
    for k in range(TOP):
        named = named | (lanes == span_routes[:, k : k + 1].astype(jnp.int32))
    span_mask = (named & span_keep).astype(BF16)

    input_blocks = gather_blocks(layer_input, "tp")
    grad_blocks = gather_blocks(after(cotangent, input_blocks), "tp")
    input_values = jnp.concatenate(input_blocks, axis=0)

    def to_owners(matrix):
        return matrix.reshape(ep_count, shared_hidden, slice_rows)

    shared_own = jnp.concatenate(
        [to_owners(shared_gate.T), to_owners(shared_up.T), to_owners(shared_down)], axis=1
    )
    shared_own = after(shared_own, dense_full)
    shared_span = lax.all_to_all(shared_own, "ep", split_axis=0, concat_axis=0, tiled=True)
    freqs = THETA ** (-(jnp.arange(HD // 2).astype(F32) * 2.0) / HD)
    angles = position.astype(F32)[:, None] * freqs[None, :]
    angles = jnp.concatenate([angles, angles], axis=-1)
    cosine = jnp.cos(angles)[:, None, :]
    sine = jnp.sin(angles)[:, None, :]
    input_values = after(input_values, picks, cosine, sine).astype(F32)
    entry_unit, entry_inverse = norm_parts(input_values)
    entry_normed = (entry_unit * entry_full).astype(BF16)
    in_lin = dot_nn(entry_normed, in_weight) + bias_full
    query_heads = in_lin[:, :head_cols].reshape(group_rows, head_count, HD)
    key_heads = in_lin[:, head_cols : 2 * head_cols].reshape(group_rows, head_count, HD)
    query_rot = (query_heads * cosine + rotate(query_heads) * sine).astype(BF16)
    key_rot = (key_heads * cosine + rotate(key_heads) * sine).astype(BF16)
    value_heads = in_lin[:, 2 * head_cols :].astype(BF16).reshape(group_rows, head_count, HD)
    score_scale = HD ** (-0.5)
    causal = position[:, None] >= position[None, :]

    def score_matrix():
        raw_scores = jnp.einsum("qhd,khd->hqk", query_rot, key_rot, preferred_element_type=F32)
        return jnp.where(causal[None], raw_scores * score_scale, -1e30)

    scores = score_matrix()
    top_score = jnp.max(scores, axis=-1, keepdims=True)
    log_total = top_score + jnp.log(jnp.sum(jnp.exp(scores - top_score), axis=-1, keepdims=True))
    attn_probs = jnp.exp(scores - log_total).astype(BF16)
    context = jnp.einsum("hqk,khd->qhd", attn_probs, value_heads, preferred_element_type=F32)
    context_low = context.astype(BF16).reshape(group_rows, head_cols)
    head_blocks = split_rows(dot_nn(context_low, out_weight).astype(BF16), tp_count)
    attention_parts = send_blocks(head_blocks, "tp")

    shared_span = after(shared_span, head_blocks)
    if dp_count == 2:
        shared_other = swapped(shared_span, "dp", 1)
        shared_parts = in_order(shared_span, shared_other, lax.axis_index("dp"), 1)
    else:
        shared_parts = lax.all_gather(shared_span, "dp", axis=0, tiled=True)
    shared_parts = shared_parts.reshape(part_count, 3, shared_hidden, slice_rows)
    shared_parts = shared_parts.transpose(1, 2, 0, 3).reshape(3, shared_hidden, width)

    def stack_hidden(expert_rows, shared_rows):
        padded = [jnp.pad(rows, ((0, seg - rows.shape[0]), (0, 0))) for rows in expert_rows]
        padded.append(jnp.pad(shared_rows, ((0, seg - shared_hidden), (0, 0))))
        return padded

    gate_rows = stack_hidden([expert_gate[j].T for j in range(local_experts)], shared_parts[0])
    up_rows = stack_hidden([expert_up[j].T for j in range(local_experts)], shared_parts[1])
    down_rows = stack_hidden([expert_down[j] for j in range(local_experts)], shared_parts[2])
    first_weight = jnp.concatenate(
        [rows for pair in zip(gate_rows, up_rows) for rows in pair], axis=0
    )
    down_weight = jnp.concatenate(down_rows, axis=0)

    grad_blocks = after(grad_blocks, head_blocks)
    group_upstream = jnp.concatenate(grad_blocks, axis=0)
    near = swapped(group_upstream, "ep", 2)

    attention_parts = after(attention_parts, near)
    if dp_count == 2:
        attention_parts = after(attention_parts, shared_other)
    attention_own = add_up([head_blocks[0], *attention_parts])
    hidden_state = input_values[:own_rows] + own_keep * attention_own
    middle_unit, middle_inverse = norm_parts(hidden_state)
    middle_normed = (middle_unit * middle_full).astype(BF16)

    span_normed = lax.all_gather(middle_normed, ("ep", "tp"), axis=0, tiled=True)
    sibling, far = swapped(group_upstream, "ep", 1), swapped(near, "ep", 1)

    def upstream_moves(_, place, turn):
        moves = []
        for k in range(4):
            for j in range(tp_count):
                block = (place ^ k) * tp_count + lax.rem(turn - j + tp_count, tp_count)
                start = pl.multiple_of(block * own_rows, own_rows)
                moves.append((k, pl.ds(j * own_rows, own_rows), 0, pl.ds(start, own_rows)))
        return moves

    upstream = move_blocks(
        upstream_moves,
        [jax.ShapeDtypeStruct((span_rows, width), BF16)],
        [group_upstream, sibling, near, far],
        "order_rows",
    )[0]

    own_logits = dot_nn(middle_normed, small_full)
    expert_probs = jax.nn.softmax(own_logits[:, :expert_count], axis=-1)
    switch_value = jax.nn.sigmoid(own_logits[:, expert_count : expert_count + 1])
    own_routes = lax.dynamic_slice_in_dim(routes, tp_index * own_rows, own_rows, 0)
    route_mask = jnp.any(
        own_routes[:, :, None] == jnp.arange(expert_count)[None, None, :], axis=1
    ).astype(F32)

    first_weight, down_weight = after((first_weight, down_weight), middle_normed)
    span_mask = after(span_mask, expert_probs, switch_value, route_mask)
    small_rows_low = small_full.T
    shared_operands = (span_normed, upstream, span_mask, picks, small_rows_low, first_weight, down_weight)
    sibling_back, chip_back, *made = run_experts(
        (ep_index ^ 3, ep_index ^ 2), tp_index, tp_count, expert_count, *shared_operands, ()
    )
    chip_sum = add_up([chip_back, swapped(sibling_back, "ep", 1)]).astype(BF16)
    from_chip = swapped(chip_sum, "ep", 2)
    sibling_back, group_back, first_grad, hidden_gated = run_experts(
        (after(ep_index ^ 1, chip_sum), ep_index),
        tp_index,
        tp_count,
        expert_count,
        *shared_operands,
        made,
    )
    from_core = [swapped(block, "ep", 1) for block in split_rows(sibling_back, tp_count)]
    down_grad = dot_tn(hidden_gated, upstream).astype(BF16)

    def last_moves(*_):
        return [
            (0, pl.ds(j * seg, hidden), 0, pl.ds(j * hidden, hidden)) for j in range(local_experts)
        ]

    last_own = move_blocks(
        last_moves,
        [jax.ShapeDtypeStruct((local_experts * hidden, width), BF16)],
        [down_grad],
        "down_rows",
    )[0]
    last_other = swapped_or_none(last_own, "dp")
    from_core = after(from_core, last_own)
    back_blocks = [
        add_up(blocks)
        for blocks in zip(
            split_rows(group_back, tp_count), from_core, split_rows(from_chip, tp_count)
        )
    ]
    back_blocks = [back_blocks[0]] + [block.astype(BF16) for block in back_blocks[1:]]
    back_parts = send_blocks(back_blocks, "tp")

    first_grad = after(first_grad, back_blocks)
    first_weight_grad = dot_tn(first_grad, span_normed).astype(BF16)
    shared_size = width // dp_count

    def first_moves(place, *_):
        moves = [
            (0, pl.ds((2 * j + part) * seg, hidden), part, pl.ds(j * hidden, hidden))
            for part in range(2)
            for j in range(local_experts)
        ]
        starts = (place, 1 - place) if dp_count == 2 else (0, 0)
        for k, start in enumerate(starts):
            columns = pl.ds(0, width)
            if dp_count == 2:
                columns = pl.ds(pl.multiple_of(start * shared_size, LANES), shared_size)
            for part, (array, base) in enumerate(
                ((0, 2 * local_experts * seg), (0, (2 * local_experts + 1) * seg), (1, local_experts * seg))
            ):
                moves.append(
                    (
                        array,
                        (pl.ds(base, shared_hidden), columns),
                        2 + k,
                        pl.ds(part * shared_hidden, shared_hidden),
                    )
                )
        return moves

    shared_shape = (3 * shared_hidden, shared_size if dp_count == 2 else width)
    *first_own, shared_kept, shared_given = move_blocks(
        first_moves,
        [jax.ShapeDtypeStruct((local_experts * hidden, width), BF16)] * 2
        + [jax.ShapeDtypeStruct(shared_shape, BF16)] * 2,
        [first_weight_grad, down_grad],
        "first_rows",
    )
    first_other = [swapped_or_none(part, "dp") for part in first_own]
    hidden_gated = after(hidden_gated, first_own)
    branch = dot_nn(hidden_gated, down_weight).astype(BF16)
    branch_terms = lax.all_to_all(
        branch.reshape(ep_count, group_rows, width), "ep", split_axis=0, concat_axis=0, tiled=True
    )
    back_parts = after(back_parts, branch, shared_kept, shared_given)
    if dp_count == 2:
        back_parts = after(back_parts, last_other)

    state_grad, attention_grad_own, router_part, middle_part = run_own(
        expert_count,
        [back_blocks[0], *back_parts],
        (expert_probs, route_mask, switch_value, own_keep),
        small_rows_low,
        middle_unit,
        middle_inverse,
        middle_normed,
        cotangent,
    )
    router_part = router_part[: expert_count + 1]
    attention_grad_blocks = gather_blocks(attention_grad_own, "tp")

    if dp_count == 2:
        attention_grad_blocks = after(attention_grad_blocks, first_other[0])
    attention_grad = jnp.concatenate(attention_grad_blocks, axis=0)
    grads_other = swapped_or_none(shared_given, "dp")

    mixing_grad = dot_tn(context_low, attention_grad).astype(BF16)
    mixing_sum = lax.psum_scatter(mixing_grad, ("dp", "ep"), scatter_dimension=1, tiled=True)
    context_grad = dot_nt(attention_grad, out_weight)
    context_grad = context_grad.astype(BF16).reshape(group_rows, head_count, HD)
    probs_again = jnp.exp(score_matrix() - log_total)
    probs_low = probs_again.astype(BF16)
    value_grad = jnp.einsum("hqk,qhd->khd", probs_low, context_grad, preferred_element_type=F32)
    value_grad = value_grad.astype(BF16).reshape(group_rows, head_cols)
    prob_grads = jnp.einsum("qhd,khd->hqk", context_grad, value_heads, preferred_element_type=F32)
    row_delta = jnp.sum(probs_again * prob_grads, axis=-1, keepdims=True)
    score_grads = (probs_again * (prob_grads - row_delta)).astype(BF16)
    query_rot_grad = (
        jnp.einsum("hqk,khd->qhd", score_grads, key_rot, preferred_element_type=F32) * score_scale
    )
    key_rot_grad = (
        jnp.einsum("hqk,qhd->khd", score_grads, query_rot, preferred_element_type=F32) * score_scale
    )
    query_grad = (query_rot_grad * cosine + unrotate(query_rot_grad * sine)).astype(BF16)
    key_grad = (key_rot_grad * cosine + unrotate(key_rot_grad * sine)).astype(BF16)
    query_grad = after(query_grad, mixing_grad)
    in_grad = jnp.concatenate(
        [query_grad.reshape(group_rows, head_cols), key_grad.reshape(group_rows, head_cols), value_grad],
        axis=1,
    )
    in_grad = after(in_grad, branch_terms)
    bias_grad = jnp.sum(in_grad.astype(F32), axis=0)
    entry_part = dot_nt(in_grad, in_weight)
    entry_blocks = split_rows(entry_part.astype(BF16), tp_count)
    entry_parts = send_blocks(entry_blocks, "tp")
    if dp_count == 2:
        shared_mine = add_up([shared_kept, grads_other]).astype(BF16)
    else:
        shared_mine = lax.psum_scatter(shared_kept, "dp", scatter_dimension=1, tiled=True)
    shared_mine = shared_mine.reshape(3 * shared_hidden, ep_count, slice_rows).transpose(1, 0, 2)
    shared_back = lax.all_to_all(shared_mine, "ep", split_axis=0, concat_axis=0, tiled=True)
    shared_back = shared_back.reshape(ep_count, 3, shared_hidden, slice_rows).astype(F32)
    branch_blocks = []
    for j in range(tp_count):
        start = ((tp_index - j) % tp_count) * own_rows
        rows = lax.dynamic_slice_in_dim(branch_terms, start, own_rows, 1)
        branch_blocks.append(jnp.sum(rows.astype(F32), axis=0))
    branch_blocks = [branch_blocks[0]] + [block.astype(BF16) for block in branch_blocks[1:]]
    branch_parts = send_blocks(branch_blocks, "tp")
    last_sum = whole_sum(last_own, last_other, "dp").reshape(local_experts, hidden, width)
    first_sum = [whole_sum(first_own[0], first_other[0], "dp")]
    entry_parts = after(entry_parts, branch_parts, shared_mine, last_sum, first_sum)
    if dp_count == 2:
        first_other[1] = after(first_other[1], entry_parts)
    first_sum.append(whole_sum(first_own[1], first_other[1], "dp"))
    first_sum = [part.reshape(local_experts, hidden, width) for part in first_sum]
    entry_own = add_up([entry_blocks[0], *entry_parts])
    input_gradient = state_grad + norm_back(
        entry_own, entry_full, entry_unit[:own_rows], entry_inverse[:own_rows]
    )

    entry_gain_part = jnp.sum(entry_part * entry_unit, axis=0, keepdims=True)
    small_part = ordered_sum(
        jnp.concatenate([router_part, middle_part, entry_gain_part], axis=0), "tp", branch_blocks
    )
    bias_part = bias_grad.reshape(3, head_count, part_count, -1).transpose(2, 0, 1, 3)
    bias_part = bias_part.reshape(part_count, bias_rows)
    bias_part = jnp.pad(bias_part, ((0, 0), (0, bias_depth * slice_rows - bias_rows)))
    bias_part = bias_part.reshape(part_count, bias_depth, slice_rows).transpose(1, 0, 2)
    bias_part = bias_part.reshape(bias_depth, width)
    small_part = jnp.concatenate([small_part, bias_part], axis=0)
    small_high, small_low = split_pair(small_part)
    small_count = small_part.shape[0]
    small_cols = jnp.concatenate(
        [
            jnp.pad(small_high, ((0, half - small_count), (0, 0))),
            jnp.pad(small_low, ((0, half - small_count), (0, 0))),
        ],
        axis=0,
    ).T
    dense_grad = jnp.concatenate(
        [
            dot_tn(entry_normed, in_grad).astype(BF16),
            small_cols,
        ],
        axis=1,
    )
    if dp_count == 2:
        dense_grad = after(dense_grad, grads_other)
    dense_sum = lax.psum_scatter(
        dense_grad, ("dp", "ep"), scatter_dimension=0, tiled=True
    ).astype(F32)
    small_sum = dense_sum[:, 3 * head_cols : 3 * head_cols + half] + dense_sum[:, 3 * head_cols + half :]
    bias_sum = small_sum[:, expert_count + 3 : expert_count + 3 + bias_depth]
    bias_sum = bias_sum.T.reshape(-1)[:bias_rows].reshape(heads_bias.shape)

    layer_output = (hidden_state + add_up([branch_blocks[0], *branch_parts])).astype(BF16)
    def by_columns(rows):
        return rows.transpose(2, 0, 1).reshape(slice_rows, ep_count * shared_hidden)

    return (
        layer_output,
        input_gradient,
        dense_sum[:, :head_cols],
        dense_sum[:, head_cols : 2 * head_cols],
        dense_sum[:, 2 * head_cols : 3 * head_cols],
        mixing_sum.astype(F32),
        bias_sum,
        small_sum[:, expert_count + 2],
        small_sum[:, expert_count + 1],
        small_sum[:, :expert_count],
        small_sum[:, expert_count],
        by_columns(shared_back[:, 0]),
        by_columns(shared_back[:, 1]),
        shared_back[:, 2].reshape(ep_count * shared_hidden, slice_rows),
        first_sum[0].transpose(0, 2, 1),
        first_sum[1].transpose(0, 2, 1),
        last_sum,
    )


def solution(mesh):
    rows = P(("dp", "ep", "tp"), None)
    parts = P(("dp", "ep"))
    in_cols = P(("dp", "ep"), "tp")
    out_cols = P("tp", ("dp", "ep"))
    weights = (
        in_cols,
        in_cols,
        in_cols,
        out_cols,
        P(None, "tp", ("dp", "ep")),
        parts,
        parts,
        P(("dp", "ep"), None),
        parts,
        in_cols,
        in_cols,
        out_cols,
        P("ep", None, "tp"),
        P("ep", None, "tp"),
        P("ep", "tp", None),
    )
    return jax.shard_map(
        body,
        mesh=mesh,
        in_specs=(rows, rows, P(), P(), P(("dp", "ep"), None)) + weights,
        out_specs=(rows, rows) + weights,
        check_vma=False,
    )
```

```python
import jax
import jax.numpy as jnp
from jax import lax
from jax.experimental import pallas as pl
from jax.experimental.pallas import tpu as pltpu
from jax.sharding import PartitionSpec as P

HD = 128
TOP = 4
EPS = 1e-06
THETA = 1000000.0
LANES = 128
F32 = jnp.float32
BF16 = jnp.bfloat16


def dot_nn(left, right):
    return lax.dot_general(left, right, (((1,), (0,)), ((), ())), preferred_element_type=F32)


def dot_nt(left, right):
    return lax.dot_general(left, right, (((1,), (1,)), ((), ())), preferred_element_type=F32)


def dot_tn(left, right):
    return lax.dot_general(left, right, (((0,), (0,)), ((), ())), preferred_element_type=F32)


def norm_parts(values):
    inverse = lax.rsqrt(jnp.mean(values * values, axis=-1, keepdims=True) + EPS)
    return (values * inverse, inverse)


def norm_back(grad_normed, gain_vector, unit_rows, inverse):
    scaled = grad_normed * gain_vector
    return inverse * (scaled - unit_rows * jnp.mean(scaled * unit_rows, axis=-1, keepdims=True))


def rotate(values):
    middle = values.shape[-1] // 2
    return jnp.concatenate([-values[..., middle:], values[..., :middle]], axis=-1)


def unrotate(values):
    middle = values.shape[-1] // 2
    return jnp.concatenate([values[..., middle:], -values[..., :middle]], axis=-1)


def split_pair(values):
    high = values.astype(BF16)
    rest = values - lax.reduce_precision(values, exponent_bits=8, mantissa_bits=7)
    return high, rest.astype(BF16)


def shifted(block, axis, step):
    count = lax.axis_size(axis)
    return lax.ppermute(block, axis, [(i, (i + step) % count) for i in range(count)])


def gather_blocks(block, axis):
    count = lax.axis_size(axis)
    return [block] + [shifted(block, axis, step) for step in range(1, count)]


def send_blocks(blocks, axis):
    return [shifted(blocks[step], axis, -step) for step in range(1, len(blocks))]


def split_rows(values, count):
    rows = values.shape[0] // count
    return [values[j * rows : (j + 1) * rows] for j in range(count)]


def add_up(values):
    total = values[0].astype(F32)
    for value in values[1:]:
        total = total + value.astype(F32)
    return total


def ordered_sum(values, axis):
    count = lax.axis_size(axis)
    place = lax.axis_index(axis)
    blocks = gather_blocks(values, axis)
    total = None
    for j in range(count):
        steps = (place - j) % count
        block = blocks[0]
        for step in range(1, count):
            block = jnp.where(steps == step, blocks[step], block)
        total = block if total is None else total + block
    return total


def swapped_or_none(values, axis):
    return swapped(values, axis, 1) if lax.axis_size(axis) == 2 else None


def whole_sum(values, other, axis):
    if other is not None:
        return values.astype(F32) + other.astype(F32)
    return lax.psum(values, axis).astype(F32)


def swapped(values, axis, bit):
    count = lax.axis_size(axis)
    return lax.ppermute(values, axis, [(i, i ^ bit) for i in range(count)])


def in_order(values, other, place, bit):
    first = (place & bit) == 0
    return jnp.concatenate(
        [jnp.where(first, values, other), jnp.where(first, other, values)], axis=0
    )


def after(value, *others):
    return lax.optimization_barrier((value,) + others)[0]


def move_blocks(moves, shapes, arrays, name):
    count = len(moves(0, 0, 0))

    def shape_of(move):
        index = move[1] if isinstance(move[1], tuple) else (move[1],)
        whole = arrays[move[0]].shape
        return tuple(i.size for i in index) + whole[len(index) :]

    def kernel(*refs):
        given, made = refs[: len(arrays)], refs[len(arrays) : len(arrays) + len(shapes)]
        held, (came, gone) = refs[len(arrays) + len(shapes) : -2], refs[-2:]
        todo = moves(lax.axis_index("dp"), lax.axis_index("ep"), lax.axis_index("tp"))
        loads = [
            pltpu.make_async_copy(given[move[0]].at[move[1]], held[k], came.at[k])
            for k, move in enumerate(todo)
        ]
        stores = [
            pltpu.make_async_copy(held[k], made[move[2]].at[move[3]], gone.at[k])
            for k, move in enumerate(todo)
        ]
        for load in loads:
            load.start()
        for load, store in zip(loads, stores):
            load.wait()
            store.start()
        for store in stores:
            store.wait()

    size = sum(2 * shape.size * shape.dtype.itemsize for shape in shapes)
    anywhere = pl.BlockSpec(memory_space=pl.ANY)
    return pl.pallas_call(
        kernel,
        in_specs=[anywhere] * len(arrays),
        out_specs=[anywhere] * len(shapes),
        out_shape=shapes,
        scratch_shapes=[pltpu.VMEM(shape_of(move), BF16) for move in moves(0, 0, 0)]
        + [pltpu.SemaphoreType.DMA((count,))] * 2,
        compiler_params=pltpu.CompilerParams(vmem_limit_bytes=24 << 20),
        cost_estimate=pl.CostEstimate(flops=0, bytes_accessed=size, transcendentals=0),
        name=name,
    )(*arrays)


def expert_kernel(
    half_count,
    expert_count,
    place_ref,
    rows_ref,
    upstream_ref,
    mask_ref,
    pick_ref,
    router_ref,
    first_ref,
    down_ref,
    *refs,
):
    *back_refs, grad_ref, gated_ref, gate_scratch, extra_scratch, back_scratch = refs[-7:]
    rows, width = rows_ref.shape
    segments = gate_scratch.shape[0]
    seg = down_ref.shape[0] // segments
    logits = dot_nt(rows_ref[...], router_ref[...])
    lane = lax.broadcasted_iota(jnp.int32, logits.shape, 1)
    routed = lane < expert_count
    top = jnp.max(jnp.where(routed, logits, -1e30), axis=1, keepdims=True)
    powers = jnp.where(routed, jnp.exp(jnp.where(routed, logits, top) - top), 0.0)
    probs = powers / jnp.sum(powers, axis=1, keepdims=True)
    switch = jax.nn.sigmoid(logits)
    gates = jnp.where(routed, probs, jnp.where(lane == expert_count, switch, 0.0))
    gates = gates * mask_ref[...].astype(F32)
    for j in range(segments):
        column = jnp.sum(gates * pick_ref[j : j + 1, :], axis=1, keepdims=True)
        gate_scratch[j] = jnp.broadcast_to(column, (rows, LANES))
    extra_scratch[...] = jnp.zeros_like(extra_scratch)
    back_scratch[...] = dot_nt(upstream_ref[...], down_ref[...])

    @pl.loop(0, segments)
    def _(j):
        low = pl.multiple_of(j * seg, LANES)
        first = pl.multiple_of(2 * j * seg, LANES)
        second = pl.multiple_of((2 * j + 1) * seg, LANES)
        gate = jnp.concatenate([gate_scratch[j]] * (seg // LANES), axis=1)
        pre = dot_nt(rows_ref[...], first_ref[pl.ds(first, 2 * seg), :])
        pre_gate, pre_up = pre[:, :seg], pre[:, seg:]
        back_lin = back_scratch[:, pl.ds(low, seg)]
        sigmoid = jax.nn.sigmoid(pre_gate)
        act = pre_gate * sigmoid
        hidden_low = (act * pre_up).astype(BF16).astype(F32)
        gated_ref[:, pl.ds(low, seg)] = (gate * hidden_low).astype(BF16)
        total = jnp.sum(hidden_low * back_lin, axis=1, keepdims=True)
        total_high = total.astype(BF16).astype(F32)
        extra_scratch[...] += total_high * pick_ref[pl.ds(j, 1), :]
        extra_scratch[...] += (total - total_high) * pick_ref[pl.ds(segments + j, 1), :]
        hidden_grad = gate * back_lin
        grad_ref[:, pl.ds(second, seg)] = (hidden_grad * act).astype(BF16)
        slope = sigmoid * (1.0 + pre_gate * (1.0 - sigmoid))
        grad_ref[:, pl.ds(first, seg)] = (hidden_grad * pre_up * slope).astype(BF16)

    count = rows // half_count
    place = place_ref[pl.num_programs(0)]

    def store(columns, values):
        for b in range(half_count):
            slot = lax.rem(place - b + half_count, half_count)
            start = pl.multiple_of(slot * count, count)
            part = values[b * count : (b + 1) * count].astype(BF16)
            for k, back_ref in enumerate(back_refs):

                @pl.when(pl.program_id(0) == k)
                def _(back_ref=back_ref, part=part, start=start):
                    back_ref[pl.ds(start, count), columns] = part


    step = width // 2

    @pl.loop(0, width // step)
    def _(n):
        columns = pl.ds(pl.multiple_of(n * step, step), step)
        store(columns, dot_nn(grad_ref[...], first_ref[:, columns]))

    store(pl.ds(width, LANES), extra_scratch[...])


def own_kernel(expert_count, *refs):
    (first_ref, *part_refs) = refs[:-14]
    (
        probs_ref, mask_ref, switch_ref, keep_ref, small_ref, unit_ref, inverse_ref, normed_ref,
        upstream_ref, state_ref, low_ref, router_ref, middle_ref, total_ref,
    ) = refs[-14:]
    width = unit_ref.shape[1]
    total_ref[...] = first_ref[...]
    for part_ref in part_refs:
        total_ref[...] += part_ref[...].astype(F32)
    sums = total_ref[:, width:]
    sums = sums + pltpu.roll(sums, LANES // 2, axis=1)
    probs, mask = probs_ref[...], mask_ref[...]
    keep, switch = keep_ref[:, :1], switch_ref[:, :1]
    lane = lax.broadcasted_iota(jnp.int32, sums.shape, 1)
    prob_grad = jnp.where(lane < expert_count, keep * mask * sums, 0.0)
    mean = jnp.sum(probs * prob_grad, axis=1, keepdims=True)
    score = jnp.where(lane < expert_count, probs * (prob_grad - mean), 0.0)
    score = jnp.where(lane == expert_count, keep * sums * switch * (1.0 - switch), score)
    high = score.astype(BF16)
    low = (score - high.astype(F32)).astype(BF16)
    small = small_ref[...]
    normed_total = total_ref[:, :width] + dot_nn(high, small) + dot_nn(low, small)
    normed = normed_ref[...]
    router_ref[...] = dot_tn(high, normed) + dot_tn(low, normed)
    unit = unit_ref[...]
    middle_ref[...] = jnp.sum(normed_total * unit, axis=0, keepdims=True)
    gain = small[expert_count + 2 : expert_count + 3, :].astype(F32)
    state = upstream_ref[...].astype(F32) + norm_back(normed_total, gain, unit, inverse_ref[:, :1])
    state_ref[...] = state
    low_ref[...] = (keep * state).astype(BF16)


def run_own(expert_count, blocks, scores, small, unit, inverse, normed, upstream):
    rows, width = unit.shape
    wide = lambda column: jnp.broadcast_to(column, (rows, LANES))
    probs, mask, switch, keep = scores
    pad = lambda values: jnp.pad(values, ((0, 0), (0, LANES - values.shape[1])))
    operands = [
        *blocks, pad(probs), pad(mask), wide(switch), wide(keep), small, unit, wide(inverse), normed, upstream,
    ]
    return pl.pallas_call(
        lambda *refs: own_kernel(expert_count, *refs),
        in_specs=[pl.BlockSpec(memory_space=pltpu.VMEM)] * len(operands),
        out_specs=[pl.BlockSpec(memory_space=pltpu.VMEM)] * 4,
        out_shape=[
            jax.ShapeDtypeStruct((rows, width), F32),
            jax.ShapeDtypeStruct((rows, width), BF16),
            jax.ShapeDtypeStruct((LANES, width), F32),
            jax.ShapeDtypeStruct((1, width), F32),
        ],
        scratch_shapes=[pltpu.VMEM((rows, width + LANES), F32)],
        compiler_params=pltpu.CompilerParams(vmem_limit_bytes=24 << 20),
        cost_estimate=pl.CostEstimate(
            flops=60 * 8 * rows * width * LANES, bytes_accessed=24 * rows * width, transcendentals=0
        ),
        name="own_rows",
    )(*operands)


def run_experts(
    groups, tp_index, tp_count, expert_count, rows, upstream, mask, picks, router, first, down, earlier
):
    span_rows, width = rows.shape
    steps = len(groups)
    hidden_all = down.shape[0]
    segments = picks.shape[0] // 2
    group_rows = mask.shape[0] // 4
    here = lambda k, place: (place[k], 0)
    fixed = lambda k, place: (0, 0)

    def whole(array):
        return pl.BlockSpec(array.shape, fixed, pipeline_mode=pl.Buffered(1))

    in_specs = [
        pl.BlockSpec((group_rows, width), here),
        pl.BlockSpec((group_rows, width), here),
        pl.BlockSpec((group_rows, LANES), here),
        whole(picks),
        whole(router),
        whole(first),
        whole(down),
    ] + [pl.BlockSpec(memory_space=pl.ANY)] * len(earlier)
    flops = 2 * steps * group_rows * width * 5 * hidden_all
    return pl.pallas_call(
        lambda *refs: expert_kernel(tp_count, expert_count, *refs),
        grid_spec=pltpu.PrefetchScalarGridSpec(
            num_scalar_prefetch=1,
            grid=(steps,),
            in_specs=in_specs,
            out_specs=[pl.BlockSpec((group_rows, width + LANES), fixed)] * 2
            + [
                pl.BlockSpec((group_rows, 2 * hidden_all), here),
                pl.BlockSpec((group_rows, hidden_all), here),
            ],
            scratch_shapes=[
                pltpu.VMEM((segments, group_rows, LANES), F32),
                pltpu.VMEM((group_rows, LANES), F32),
                pltpu.VMEM((group_rows, hidden_all), F32),
            ],
        ),
        out_shape=[jax.ShapeDtypeStruct((group_rows, width + LANES), BF16)] * 2
        + [
            jax.ShapeDtypeStruct((span_rows, 2 * hidden_all), BF16),
            jax.ShapeDtypeStruct((span_rows, hidden_all), BF16),
        ],
        input_output_aliases={8 + i: 2 + i for i in range(len(earlier))},
        compiler_params=pltpu.CompilerParams(vmem_limit_bytes=58 << 20),
        cost_estimate=pl.CostEstimate(
            flops=flops,
            bytes_accessed=2 * (first.size + down.size + steps * group_rows * (3 * width + 3 * hidden_all)),
            transcendentals=steps * group_rows * hidden_all,
        ),
        name="experts",
    )(jnp.stack([*groups, tp_index]).astype(jnp.int32), rows, upstream, mask, picks, router, first, down, *earlier)


def body(
    layer_input,
    cotangent,
    lengths,
    seq_order,
    routes,
    query_weight,
    key_weight,
    value_weight,
    mixing_weight,
    heads_bias,
    entry_gain,
    middle_gain,
    router_weight,
    shared_switch,
    shared_gate,
    shared_up,
    shared_down,
    expert_gate,
    expert_up,
    expert_down,
):
    tp_count = lax.axis_size("tp")
    ep_count = lax.axis_size("ep")
    dp_count = lax.axis_size("dp")
    part_count = dp_count * ep_count
    tp_index = lax.axis_index("tp")
    ep_index = lax.axis_index("ep")
    own_rows, width = layer_input.shape
    group_rows = own_rows * tp_count
    span_rows = group_rows * ep_count
    slice_rows = query_weight.shape[0]
    head_cols = query_weight.shape[1]
    head_count = head_cols // HD
    local_experts = expert_gate.shape[0]
    expert_count = router_weight.shape[1]
    hidden = expert_gate.shape[2]
    shared_hidden = shared_gate.shape[1] // ep_count
    segments = local_experts + 1
    seg = -(-max(hidden, shared_hidden) // LANES) * LANES

    span_lengths = jnp.take(
        lengths,
        lax.dynamic_slice_in_dim(seq_order, lax.axis_index("dp") * ep_count, ep_count, 0),
    )
    length = span_lengths[ep_index]
    own_keep = ((tp_index * own_rows + jnp.arange(own_rows)) < length).astype(F32)[:, None]
    block_of = jnp.arange(group_rows) // own_rows
    position = ((tp_index - block_of) % tp_count) * own_rows + jnp.arange(group_rows) % own_rows

    span_keep = (jnp.arange(group_rows)[None, :] < span_lengths[:, None]).reshape(span_rows, 1)
    lanes = jnp.arange(LANES)[None, :]
    column_of = jnp.concatenate(
        [ep_index * local_experts + jnp.arange(local_experts), jnp.array([expert_count])]
    )
    half = LANES // 2
    picks = jnp.concatenate([column_of, column_of + half])[:, None] == lanes
    picks = picks.astype(F32)

    bias_rows = heads_bias.size
    small = jnp.concatenate(
        [
            router_weight,
            shared_switch[:, None],
            entry_gain[:, None],
            middle_gain[:, None],
        ],
        axis=1,
    )
    bias_depth = -(-bias_rows // slice_rows)
    bias_cols = jnp.pad(heads_bias.reshape(-1), (0, bias_depth * slice_rows - bias_rows))
    bias_cols = bias_cols.reshape(bias_depth, slice_rows).T
    route_depth = -(-routes.size // slice_rows)
    route_cols = jnp.pad(routes.reshape(-1), (0, route_depth * slice_rows - routes.size))
    route_cols = route_cols.reshape(route_depth, slice_rows).T.astype(BF16)
    small = jnp.concatenate([small, bias_cols, route_cols], axis=1)
    small = jnp.pad(small, ((0, 0), (0, LANES - small.shape[1])))
    dense_own = jnp.concatenate(
        [query_weight, key_weight, value_weight, small], axis=1
    )
    dense_full = lax.all_gather(dense_own, ("dp", "ep"), axis=0, tiled=True)
    in_weight = dense_full[:, : 3 * head_cols]
    small_full = dense_full[:, 3 * head_cols :]
    out_weight = lax.all_gather(
        after(mixing_weight, dense_full), ("dp", "ep"), axis=1, tiled=True
    )
    small_rows = small_full[:, : expert_count + 3].astype(F32).T
    entry_full = small_rows[expert_count + 1][None]
    middle_full = small_rows[expert_count + 2][None]
    bias_full = small_full[:, expert_count + 3 : expert_count + 3 + bias_depth]
    bias_full = bias_full.reshape(part_count, slice_rows, bias_depth).transpose(0, 2, 1)
    bias_full = bias_full.reshape(part_count, -1)[:, :bias_rows]
    bias_full = bias_full.reshape((part_count,) + heads_bias.shape).transpose(1, 2, 0, 3)
    bias_full = bias_full.reshape(1, 3 * head_cols).astype(F32)

    route_at = expert_count + 3 + bias_depth
    span_routes = lax.dynamic_slice_in_dim(
        small_full[:, route_at : route_at + route_depth],
        lax.axis_index("dp") * ep_count * slice_rows,
        ep_count * slice_rows,
        0,
    )
    span_routes = span_routes.reshape(ep_count, slice_rows, route_depth).transpose(0, 2, 1)
    span_routes = span_routes.reshape(ep_count, -1)[:, : routes.size].reshape(span_rows, TOP)
    named = lanes == expert_count
    for k in range(TOP):
        named = named | (lanes == span_routes[:, k : k + 1].astype(jnp.int32))
    span_mask = (named & span_keep).astype(BF16)

    input_blocks = gather_blocks(layer_input, "tp")
    grad_blocks = gather_blocks(after(cotangent, input_blocks), "tp")
    input_values = jnp.concatenate(input_blocks, axis=0)

    def to_owners(matrix):
        return matrix.reshape(ep_count, shared_hidden, slice_rows)

    shared_own = jnp.concatenate(
        [to_owners(shared_gate.T), to_owners(shared_up.T), to_owners(shared_down)], axis=1
    )
    shared_own = after(shared_own, dense_full)
    shared_span = lax.all_to_all(shared_own, "ep", split_axis=0, concat_axis=0, tiled=True)
    freqs = THETA ** (-(jnp.arange(HD // 2).astype(F32) * 2.0) / HD)
    angles = position.astype(F32)[:, None] * freqs[None, :]
    angles = jnp.concatenate([angles, angles], axis=-1)
    cosine = jnp.cos(angles)[:, None, :]
    sine = jnp.sin(angles)[:, None, :]
    input_values = after(input_values, picks, cosine, sine).astype(F32)
    entry_unit, entry_inverse = norm_parts(input_values)
    entry_normed = (entry_unit * entry_full).astype(BF16)
    in_lin = dot_nn(entry_normed, in_weight) + bias_full
    query_heads = in_lin[:, :head_cols].reshape(group_rows, head_count, HD)
    key_heads = in_lin[:, head_cols : 2 * head_cols].reshape(group_rows, head_count, HD)
    query_rot = (query_heads * cosine + rotate(query_heads) * sine).astype(BF16)
    key_rot = (key_heads * cosine + rotate(key_heads) * sine).astype(BF16)
    value_heads = in_lin[:, 2 * head_cols :].astype(BF16).reshape(group_rows, head_count, HD)
    score_scale = HD ** (-0.5)
    causal = position[:, None] >= position[None, :]

    def score_matrix():
        raw_scores = jnp.einsum("qhd,khd->hqk", query_rot, key_rot, preferred_element_type=F32)
        return jnp.where(causal[None], raw_scores * score_scale, -1e30)

    scores = score_matrix()
    top_score = jnp.max(scores, axis=-1, keepdims=True)
    log_total = top_score + jnp.log(jnp.sum(jnp.exp(scores - top_score), axis=-1, keepdims=True))
    attn_probs = jnp.exp(scores - log_total).astype(BF16)
    context = jnp.einsum("hqk,khd->qhd", attn_probs, value_heads, preferred_element_type=F32)
    context_low = context.astype(BF16).reshape(group_rows, head_cols)
    head_blocks = split_rows(dot_nn(context_low, out_weight).astype(BF16), tp_count)
    attention_parts = send_blocks(head_blocks, "tp")

    shared_span = after(shared_span, head_blocks)
    if dp_count == 2:
        shared_other = swapped(shared_span, "dp", 1)
        shared_parts = in_order(shared_span, shared_other, lax.axis_index("dp"), 1)
    else:
        shared_parts = lax.all_gather(shared_span, "dp", axis=0, tiled=True)
    shared_parts = shared_parts.reshape(part_count, 3, shared_hidden, slice_rows)
    shared_parts = shared_parts.transpose(1, 2, 0, 3).reshape(3, shared_hidden, width)

    def stack_hidden(expert_rows, shared_rows):
        padded = [jnp.pad(rows, ((0, seg - rows.shape[0]), (0, 0))) for rows in expert_rows]
        padded.append(jnp.pad(shared_rows, ((0, seg - shared_hidden), (0, 0))))
        return padded

    gate_rows = stack_hidden([expert_gate[j].T for j in range(local_experts)], shared_parts[0])
    up_rows = stack_hidden([expert_up[j].T for j in range(local_experts)], shared_parts[1])
    down_rows = stack_hidden([expert_down[j] for j in range(local_experts)], shared_parts[2])
    first_weight = jnp.concatenate(
        [rows for pair in zip(gate_rows, up_rows) for rows in pair], axis=0
    )
    down_weight = jnp.concatenate(down_rows, axis=0)

    grad_blocks = after(grad_blocks, head_blocks)
    group_upstream = jnp.concatenate(grad_blocks, axis=0)
    near = swapped(group_upstream, "ep", 2)

    attention_parts = after(attention_parts, near)
    if dp_count == 2:
        attention_parts = after(attention_parts, shared_other)
    attention_own = add_up([head_blocks[0], *attention_parts])
    hidden_state = input_values[:own_rows] + own_keep * attention_own
    middle_unit, middle_inverse = norm_parts(hidden_state)
    middle_normed = (middle_unit * middle_full).astype(BF16)

    span_normed = lax.all_gather(middle_normed, ("ep", "tp"), axis=0, tiled=True)
    sibling, far = swapped(group_upstream, "ep", 1), swapped(near, "ep", 1)

    def upstream_moves(_, place, turn):
        moves = []
        for k in range(4):
            for j in range(tp_count):
                block = (place ^ k) * tp_count + lax.rem(turn - j + tp_count, tp_count)
                start = pl.multiple_of(block * own_rows, own_rows)
                moves.append((k, pl.ds(j * own_rows, own_rows), 0, pl.ds(start, own_rows)))
        return moves

    upstream = move_blocks(
        upstream_moves,
        [jax.ShapeDtypeStruct((span_rows, width), BF16)],
        [group_upstream, sibling, near, far],
        "order_rows",
    )[0]

    own_logits = dot_nn(middle_normed, small_full)
    expert_probs = jax.nn.softmax(own_logits[:, :expert_count], axis=-1)
    switch_value = jax.nn.sigmoid(own_logits[:, expert_count : expert_count + 1])
    own_routes = lax.dynamic_slice_in_dim(routes, tp_index * own_rows, own_rows, 0)
    route_mask = jnp.any(
        own_routes[:, :, None] == jnp.arange(expert_count)[None, None, :], axis=1
    ).astype(F32)

    first_weight, down_weight = after((first_weight, down_weight), middle_normed)
    span_mask = after(span_mask, expert_probs, switch_value, route_mask)
    small_rows_low = small_full.T
    shared_operands = (span_normed, upstream, span_mask, picks, small_rows_low, first_weight, down_weight)
    sibling_back, chip_back, *made = run_experts(
        (ep_index ^ 3, ep_index ^ 2), tp_index, tp_count, expert_count, *shared_operands, ()
    )
    chip_sum = add_up([chip_back, swapped(sibling_back, "ep", 1)]).astype(BF16)
    from_chip = swapped(chip_sum, "ep", 2)
    sibling_back, group_back, first_grad, hidden_gated = run_experts(
        (after(ep_index ^ 1, chip_sum), ep_index),
        tp_index,
        tp_count,
        expert_count,
        *shared_operands,
        made,
    )
    from_core = [swapped(block, "ep", 1) for block in split_rows(sibling_back, tp_count)]
    down_grad = dot_tn(hidden_gated, upstream).astype(BF16)

    def last_moves(*_):
        return [
            (0, pl.ds(j * seg, hidden), 0, pl.ds(j * hidden, hidden)) for j in range(local_experts)
        ]

    last_own = move_blocks(
        last_moves,
        [jax.ShapeDtypeStruct((local_experts * hidden, width), BF16)],
        [down_grad],
        "down_rows",
    )[0]
    last_other = swapped_or_none(last_own, "dp")
    from_core = after(from_core, last_own)
    back_blocks = [
        add_up(blocks)
        for blocks in zip(
            split_rows(group_back, tp_count), from_core, split_rows(from_chip, tp_count)
        )
    ]
    back_blocks = [back_blocks[0]] + [block.astype(BF16) for block in back_blocks[1:]]
    back_parts = send_blocks(back_blocks, "tp")

    first_grad = after(first_grad, back_blocks)
    first_weight_grad = dot_tn(first_grad, span_normed).astype(BF16)
    shared_size = width // dp_count

    def first_moves(place, *_):
        moves = [
            (0, pl.ds((2 * j + part) * seg, hidden), part, pl.ds(j * hidden, hidden))
            for part in range(2)
            for j in range(local_experts)
        ]
        starts = (place, 1 - place) if dp_count == 2 else (0, 0)
        for k, start in enumerate(starts):
            columns = pl.ds(0, width)
            if dp_count == 2:
                columns = pl.ds(pl.multiple_of(start * shared_size, LANES), shared_size)
            for part, (array, base) in enumerate(
                ((0, 2 * local_experts * seg), (0, (2 * local_experts + 1) * seg), (1, local_experts * seg))
            ):
                moves.append(
                    (
                        array,
                        (pl.ds(base, shared_hidden), columns),
                        2 + k,
                        pl.ds(part * shared_hidden, shared_hidden),
                    )
                )
        return moves

    shared_shape = (3 * shared_hidden, shared_size if dp_count == 2 else width)
    *first_own, shared_kept, shared_given = move_blocks(
        first_moves,
        [jax.ShapeDtypeStruct((local_experts * hidden, width), BF16)] * 2
        + [jax.ShapeDtypeStruct(shared_shape, BF16)] * 2,
        [first_weight_grad, down_grad],
        "first_rows",
    )
    first_other = [swapped_or_none(part, "dp") for part in first_own]
    hidden_gated = after(hidden_gated, first_own)
    branch = dot_nn(hidden_gated, down_weight).astype(BF16)
    branch_terms = lax.all_to_all(
        branch.reshape(ep_count, group_rows, width), "ep", split_axis=0, concat_axis=0, tiled=True
    )
    back_parts = after(back_parts, branch, shared_kept, shared_given)
    if dp_count == 2:
        back_parts = after(back_parts, last_other)

    state_grad, attention_grad_own, router_part, middle_part = run_own(
        expert_count,
        [back_blocks[0], *back_parts],
        (expert_probs, route_mask, switch_value, own_keep),
        small_rows_low,
        middle_unit,
        middle_inverse,
        middle_normed,
        cotangent,
    )
    router_part = router_part[: expert_count + 1]
    attention_grad_blocks = gather_blocks(attention_grad_own, "tp")

    if dp_count == 2:
        attention_grad_blocks = after(attention_grad_blocks, first_other[0])
    attention_grad = jnp.concatenate(attention_grad_blocks, axis=0)
    grads_other = swapped_or_none(shared_given, "dp")

    mixing_grad = dot_tn(context_low, attention_grad).astype(BF16)
    mixing_sum = lax.psum_scatter(mixing_grad, ("dp", "ep"), scatter_dimension=1, tiled=True)
    context_grad = dot_nt(attention_grad, out_weight)
    context_grad = context_grad.astype(BF16).reshape(group_rows, head_count, HD)
    probs_again = jnp.exp(score_matrix() - log_total)
    probs_low = probs_again.astype(BF16)
    value_grad = jnp.einsum("hqk,qhd->khd", probs_low, context_grad, preferred_element_type=F32)
    value_grad = value_grad.astype(BF16).reshape(group_rows, head_cols)
    prob_grads = jnp.einsum("qhd,khd->hqk", context_grad, value_heads, preferred_element_type=F32)
    row_delta = jnp.sum(probs_again * prob_grads, axis=-1, keepdims=True)
    score_grads = (probs_again * (prob_grads - row_delta)).astype(BF16)
    query_rot_grad = (
        jnp.einsum("hqk,khd->qhd", score_grads, key_rot, preferred_element_type=F32) * score_scale
    )
    key_rot_grad = (
        jnp.einsum("hqk,qhd->khd", score_grads, query_rot, preferred_element_type=F32) * score_scale
    )
    query_grad = (query_rot_grad * cosine + unrotate(query_rot_grad * sine)).astype(BF16)
    key_grad = (key_rot_grad * cosine + unrotate(key_rot_grad * sine)).astype(BF16)
    query_grad = after(query_grad, mixing_grad)
    in_grad = jnp.concatenate(
        [query_grad.reshape(group_rows, head_cols), key_grad.reshape(group_rows, head_cols), value_grad],
        axis=1,
    )
    branch_blocks = []
    for j in range(tp_count):
        start = ((tp_index - j) % tp_count) * own_rows
        rows = lax.dynamic_slice_in_dim(branch_terms, start, own_rows, 1)
        branch_blocks.append(jnp.sum(rows.astype(F32), axis=0))
    branch_blocks = [branch_blocks[0]] + [block.astype(BF16) for block in branch_blocks[1:]]
    branch_parts = send_blocks(branch_blocks, "tp")
    in_grad = after(in_grad, branch_blocks)
    bias_grad = jnp.sum(in_grad.astype(F32), axis=0)
    entry_part = dot_nt(in_grad, in_weight)
    entry_blocks = split_rows(entry_part.astype(BF16), tp_count)
    entry_parts = send_blocks(entry_blocks, "tp")
    if dp_count == 2:
        shared_mine = add_up([shared_kept, grads_other]).astype(BF16)
    else:
        shared_mine = lax.psum_scatter(shared_kept, "dp", scatter_dimension=1, tiled=True)
    shared_mine = shared_mine.reshape(3 * shared_hidden, ep_count, slice_rows).transpose(1, 0, 2)
    shared_back = lax.all_to_all(shared_mine, "ep", split_axis=0, concat_axis=0, tiled=True)
    shared_back = shared_back.reshape(ep_count, 3, shared_hidden, slice_rows).astype(F32)
    last_sum = whole_sum(last_own, last_other, "dp").reshape(local_experts, hidden, width)
    first_sum = [whole_sum(first_own[0], first_other[0], "dp")]
    entry_parts = after(entry_parts, branch_parts, shared_mine, last_sum, first_sum)
    if dp_count == 2:
        first_other[1] = after(first_other[1], entry_parts)
    first_sum.append(whole_sum(first_own[1], first_other[1], "dp"))
    first_sum = [part.reshape(local_experts, hidden, width) for part in first_sum]
    entry_own = add_up([entry_blocks[0], *entry_parts])
    input_gradient = state_grad + norm_back(
        entry_own, entry_full, entry_unit[:own_rows], entry_inverse[:own_rows]
    )

    entry_gain_part = jnp.sum(entry_part * entry_unit, axis=0, keepdims=True)
    small_part = jnp.concatenate([router_part, middle_part, entry_gain_part], axis=0)
    bias_part = bias_grad.reshape(3, head_count, part_count, -1).transpose(2, 0, 1, 3)
    bias_part = bias_part.reshape(part_count, bias_rows)
    bias_part = jnp.pad(bias_part, ((0, 0), (0, bias_depth * slice_rows - bias_rows)))
    bias_part = bias_part.reshape(part_count, bias_depth, slice_rows).transpose(1, 0, 2)
    bias_part = bias_part.reshape(bias_depth, width)
    small_part = jnp.concatenate([small_part, bias_part], axis=0)
    small_high, small_low = split_pair(small_part)
    small_count = small_part.shape[0]
    small_cols = jnp.concatenate(
        [
            jnp.pad(small_high, ((0, half - small_count), (0, 0))),
            jnp.pad(small_low, ((0, half - small_count), (0, 0))),
        ],
        axis=0,
    ).T
    dense_grad = jnp.concatenate(
        [
            dot_tn(entry_normed, in_grad).astype(BF16),
            small_cols,
        ],
        axis=1,
    )
    if dp_count == 2:
        dense_grad = after(dense_grad, grads_other)
    dense_grad = after(dense_grad, branch_parts[0], branch_parts[-1])
    dense_sum = lax.psum_scatter(
        dense_grad, ("dp", "ep"), scatter_dimension=0, tiled=True
    ).astype(F32)
    small_sum = dense_sum[:, 3 * head_cols : 3 * head_cols + half] + dense_sum[:, 3 * head_cols + half :]
    tp_sum = ordered_sum(small_sum[:, : expert_count + 3].T, "tp")
    bias_sum = small_sum[:, expert_count + 3 : expert_count + 3 + bias_depth]
    bias_sum = bias_sum.T.reshape(-1)[:bias_rows].reshape(heads_bias.shape)

    layer_output = (hidden_state + add_up([branch_blocks[0], *branch_parts])).astype(BF16)
    def by_columns(rows):
        return rows.transpose(2, 0, 1).reshape(slice_rows, ep_count * shared_hidden)

    return (
        layer_output,
        input_gradient,
        dense_sum[:, :head_cols],
        dense_sum[:, head_cols : 2 * head_cols],
        dense_sum[:, 2 * head_cols : 3 * head_cols],
        mixing_sum.astype(F32),
        bias_sum,
        tp_sum[expert_count + 2],
        tp_sum[expert_count + 1],
        tp_sum[:expert_count].T,
        tp_sum[expert_count],
        by_columns(shared_back[:, 0]),
        by_columns(shared_back[:, 1]),
        shared_back[:, 2].reshape(ep_count * shared_hidden, slice_rows),
        first_sum[0].transpose(0, 2, 1),
        first_sum[1].transpose(0, 2, 1),
        last_sum,
    )


def solution(mesh):
    rows = P(("dp", "ep", "tp"), None)
    parts = P(("dp", "ep"))
    in_cols = P(("dp", "ep"), "tp")
    out_cols = P("tp", ("dp", "ep"))
    weights = (
        in_cols,
        in_cols,
        in_cols,
        out_cols,
        P(None, "tp", ("dp", "ep")),
        parts,
        parts,
        P(("dp", "ep"), None),
        parts,
        in_cols,
        in_cols,
        out_cols,
        P("ep", None, "tp"),
        P("ep", None, "tp"),
        P("ep", "tp", None),
    )
    return jax.shard_map(
        body,
        mesh=mesh,
        in_specs=(rows, rows, P(), P(), P(("dp", "ep"), None)) + weights,
        out_specs=(rows, rows) + weights,
        check_vma=False,
    )
```

```python
import jax
import jax.numpy as jnp
from jax import lax
from jax.experimental import pallas as pl
from jax.experimental.pallas import tpu as pltpu
from jax.sharding import PartitionSpec as P

HD = 128
TOP = 4
EPS = 1e-06
THETA = 1000000.0
LANES = 128
F32 = jnp.float32
BF16 = jnp.bfloat16


def dot_nn(left, right):
    return lax.dot_general(left, right, (((1,), (0,)), ((), ())), preferred_element_type=F32)


def dot_nt(left, right):
    return lax.dot_general(left, right, (((1,), (1,)), ((), ())), preferred_element_type=F32)


def dot_tn(left, right):
    return lax.dot_general(left, right, (((0,), (0,)), ((), ())), preferred_element_type=F32)


def norm_parts(values):
    inverse = lax.rsqrt(jnp.mean(values * values, axis=-1, keepdims=True) + EPS)
    return (values * inverse, inverse)


def norm_back(grad_normed, gain_vector, unit_rows, inverse):
    scaled = grad_normed * gain_vector
    return inverse * (scaled - unit_rows * jnp.mean(scaled * unit_rows, axis=-1, keepdims=True))


def rotate(values):
    middle = values.shape[-1] // 2
    return jnp.concatenate([-values[..., middle:], values[..., :middle]], axis=-1)


def unrotate(values):
    middle = values.shape[-1] // 2
    return jnp.concatenate([values[..., middle:], -values[..., :middle]], axis=-1)


def split_pair(values):
    high = values.astype(BF16)
    rest = values - lax.reduce_precision(values, exponent_bits=8, mantissa_bits=7)
    return high, rest.astype(BF16)


def shifted(block, axis, step):
    count = lax.axis_size(axis)
    return lax.ppermute(block, axis, [(i, (i + step) % count) for i in range(count)])


def gather_blocks(block, axis):
    count = lax.axis_size(axis)
    return [block] + [shifted(block, axis, step) for step in range(1, count)]


def send_blocks(blocks, axis):
    return [shifted(blocks[step], axis, -step) for step in range(1, len(blocks))]


def split_rows(values, count):
    rows = values.shape[0] // count
    return [values[j * rows : (j + 1) * rows] for j in range(count)]


def add_up(values):
    total = values[0].astype(F32)
    for value in values[1:]:
        total = total + value.astype(F32)
    return total


def ordered_sum(values, axis):
    count = lax.axis_size(axis)
    place = lax.axis_index(axis)
    blocks = gather_blocks(values, axis)
    total = None
    for j in range(count):
        steps = (place - j) % count
        block = blocks[0]
        for step in range(1, count):
            block = jnp.where(steps == step, blocks[step], block)
        total = block if total is None else total + block
    return total


def swapped_or_none(values, axis):
    return swapped(values, axis, 1) if lax.axis_size(axis) == 2 else None


def whole_sum(values, other, axis):
    if other is not None:
        return values.astype(F32) + other.astype(F32)
    return lax.psum(values, axis).astype(F32)


def swapped(values, axis, bit):
    count = lax.axis_size(axis)
    return lax.ppermute(values, axis, [(i, i ^ bit) for i in range(count)])


def in_order(values, other, place, bit):
    first = (place & bit) == 0
    return jnp.concatenate(
        [jnp.where(first, values, other), jnp.where(first, other, values)], axis=0
    )


def after(value, *others):
    return lax.optimization_barrier((value,) + others)[0]


def move_blocks(moves, shapes, arrays, name):
    count = len(moves(0, 0, 0))

    def shape_of(move):
        index = move[1] if isinstance(move[1], tuple) else (move[1],)
        whole = arrays[move[0]].shape
        return tuple(i.size for i in index) + whole[len(index) :]

    def kernel(*refs):
        given, made = refs[: len(arrays)], refs[len(arrays) : len(arrays) + len(shapes)]
        held, (came, gone) = refs[len(arrays) + len(shapes) : -2], refs[-2:]
        todo = moves(lax.axis_index("dp"), lax.axis_index("ep"), lax.axis_index("tp"))
        loads = [
            pltpu.make_async_copy(given[move[0]].at[move[1]], held[k], came.at[k])
            for k, move in enumerate(todo)
        ]
        stores = [
            pltpu.make_async_copy(held[k], made[move[2]].at[move[3]], gone.at[k])
            for k, move in enumerate(todo)
        ]
        for load in loads:
            load.start()
        for load, store in zip(loads, stores):
            load.wait()
            store.start()
        for store in stores:
            store.wait()

    size = sum(2 * shape.size * shape.dtype.itemsize for shape in shapes)
    anywhere = pl.BlockSpec(memory_space=pl.ANY)
    return pl.pallas_call(
        kernel,
        in_specs=[anywhere] * len(arrays),
        out_specs=[anywhere] * len(shapes),
        out_shape=shapes,
        scratch_shapes=[pltpu.VMEM(shape_of(move), BF16) for move in moves(0, 0, 0)]
        + [pltpu.SemaphoreType.DMA((count,))] * 2,
        compiler_params=pltpu.CompilerParams(vmem_limit_bytes=24 << 20),
        cost_estimate=pl.CostEstimate(flops=0, bytes_accessed=size, transcendentals=0),
        name=name,
    )(*arrays)


def expert_kernel(
    half_count,
    expert_count,
    place_ref,
    rows_ref,
    upstream_ref,
    mask_ref,
    pick_ref,
    router_ref,
    first_ref,
    down_ref,
    *refs,
):
    *back_refs, grad_ref, gated_ref, gate_scratch, extra_scratch, back_scratch = refs[-7:]
    rows, width = rows_ref.shape
    segments = gate_scratch.shape[0]
    seg = down_ref.shape[0] // segments
    logits = dot_nt(rows_ref[...], router_ref[...])
    lane = lax.broadcasted_iota(jnp.int32, logits.shape, 1)
    routed = lane < expert_count
    top = jnp.max(jnp.where(routed, logits, -1e30), axis=1, keepdims=True)
    powers = jnp.where(routed, jnp.exp(jnp.where(routed, logits, top) - top), 0.0)
    probs = powers / jnp.sum(powers, axis=1, keepdims=True)
    switch = jax.nn.sigmoid(logits)
    gates = jnp.where(routed, probs, jnp.where(lane == expert_count, switch, 0.0))
    gates = gates * mask_ref[...].astype(F32)
    for j in range(segments):
        column = jnp.sum(gates * pick_ref[j : j + 1, :], axis=1, keepdims=True)
        gate_scratch[j] = jnp.broadcast_to(column, (rows, LANES))
    extra_scratch[...] = jnp.zeros_like(extra_scratch)
    back_scratch[...] = dot_nt(upstream_ref[...], down_ref[...])

    @pl.loop(0, segments)
    def _(j):
        low = pl.multiple_of(j * seg, LANES)
        first = pl.multiple_of(2 * j * seg, LANES)
        second = pl.multiple_of((2 * j + 1) * seg, LANES)
        gate = jnp.concatenate([gate_scratch[j]] * (seg // LANES), axis=1)
        pre = dot_nt(rows_ref[...], first_ref[pl.ds(first, 2 * seg), :])
        pre_gate, pre_up = pre[:, :seg], pre[:, seg:]
        back_lin = back_scratch[:, pl.ds(low, seg)]
        sigmoid = jax.nn.sigmoid(pre_gate)
        act = pre_gate * sigmoid
        hidden_low = (act * pre_up).astype(BF16).astype(F32)
        gated_ref[:, pl.ds(low, seg)] = (gate * hidden_low).astype(BF16)
        total = jnp.sum(hidden_low * back_lin, axis=1, keepdims=True)
        total_high = total.astype(BF16).astype(F32)
        extra_scratch[...] += total_high * pick_ref[pl.ds(j, 1), :]
        extra_scratch[...] += (total - total_high) * pick_ref[pl.ds(segments + j, 1), :]
        hidden_grad = gate * back_lin
        grad_ref[:, pl.ds(second, seg)] = (hidden_grad * act).astype(BF16)
        slope = sigmoid * (1.0 + pre_gate * (1.0 - sigmoid))
        grad_ref[:, pl.ds(first, seg)] = (hidden_grad * pre_up * slope).astype(BF16)

    count = rows // half_count
    place = place_ref[pl.num_programs(0)]

    def store(columns, values):
        for b in range(half_count):
            slot = lax.rem(place - b + half_count, half_count)
            start = pl.multiple_of(slot * count, count)
            part = values[b * count : (b + 1) * count].astype(BF16)
            for k, back_ref in enumerate(back_refs):

                @pl.when(pl.program_id(0) == k)
                def _(back_ref=back_ref, part=part, start=start):
                    back_ref[pl.ds(start, count), columns] = part


    step = width // 2

    @pl.loop(0, width // step)
    def _(n):
        columns = pl.ds(pl.multiple_of(n * step, step), step)
        store(columns, dot_nn(grad_ref[...], first_ref[:, columns]))

    store(pl.ds(width, LANES), extra_scratch[...])


def own_kernel(expert_count, *refs):
    (first_ref, *part_refs) = refs[:-14]
    (
        probs_ref, mask_ref, switch_ref, keep_ref, small_ref, unit_ref, inverse_ref, normed_ref,
        upstream_ref, state_ref, low_ref, router_ref, middle_ref, total_ref,
    ) = refs[-14:]
    width = unit_ref.shape[1]
    total_ref[...] = first_ref[...]
    for part_ref in part_refs:
        total_ref[...] += part_ref[...].astype(F32)
    sums = total_ref[:, width:]
    sums = sums + pltpu.roll(sums, LANES // 2, axis=1)
    probs, mask = probs_ref[...], mask_ref[...]
    keep, switch = keep_ref[:, :1], switch_ref[:, :1]
    lane = lax.broadcasted_iota(jnp.int32, sums.shape, 1)
    prob_grad = jnp.where(lane < expert_count, keep * mask * sums, 0.0)
    mean = jnp.sum(probs * prob_grad, axis=1, keepdims=True)
    score = jnp.where(lane < expert_count, probs * (prob_grad - mean), 0.0)
    score = jnp.where(lane == expert_count, keep * sums * switch * (1.0 - switch), score)
    high = score.astype(BF16)
    low = (score - high.astype(F32)).astype(BF16)
    small = small_ref[...]
    normed_total = total_ref[:, :width] + dot_nn(high, small) + dot_nn(low, small)
    normed = normed_ref[...]
    router_ref[...] = dot_tn(high, normed) + dot_tn(low, normed)
    unit = unit_ref[...]
    middle_ref[...] = jnp.sum(normed_total * unit, axis=0, keepdims=True)
    gain = small[expert_count + 2 : expert_count + 3, :].astype(F32)
    state = upstream_ref[...].astype(F32) + norm_back(normed_total, gain, unit, inverse_ref[:, :1])
    state_ref[...] = state
    low_ref[...] = (keep * state).astype(BF16)


def run_own(expert_count, blocks, scores, small, unit, inverse, normed, upstream):
    rows, width = unit.shape
    wide = lambda column: jnp.broadcast_to(column, (rows, LANES))
    probs, mask, switch, keep = scores
    pad = lambda values: jnp.pad(values, ((0, 0), (0, LANES - values.shape[1])))
    operands = [
        *blocks, pad(probs), pad(mask), wide(switch), wide(keep), small, unit, wide(inverse), normed, upstream,
    ]
    return pl.pallas_call(
        lambda *refs: own_kernel(expert_count, *refs),
        in_specs=[pl.BlockSpec(memory_space=pltpu.VMEM)] * len(operands),
        out_specs=[pl.BlockSpec(memory_space=pltpu.VMEM)] * 4,
        out_shape=[
            jax.ShapeDtypeStruct((rows, width), F32),
            jax.ShapeDtypeStruct((rows, width), BF16),
            jax.ShapeDtypeStruct((LANES, width), F32),
            jax.ShapeDtypeStruct((1, width), F32),
        ],
        scratch_shapes=[pltpu.VMEM((rows, width + LANES), F32)],
        compiler_params=pltpu.CompilerParams(vmem_limit_bytes=24 << 20),
        cost_estimate=pl.CostEstimate(
            flops=60 * 8 * rows * width * LANES, bytes_accessed=24 * rows * width, transcendentals=0
        ),
        name="own_rows",
    )(*operands)


def run_experts(
    groups, tp_index, tp_count, expert_count, rows, upstream, mask, picks, router, first, down, earlier
):
    span_rows, width = rows.shape
    steps = len(groups)
    hidden_all = down.shape[0]
    segments = picks.shape[0] // 2
    group_rows = mask.shape[0] // 4
    here = lambda k, place: (place[k], 0)
    fixed = lambda k, place: (0, 0)

    def whole(array):
        return pl.BlockSpec(array.shape, fixed, pipeline_mode=pl.Buffered(1))

    in_specs = [
        pl.BlockSpec((group_rows, width), here),
        pl.BlockSpec((group_rows, width), here),
        pl.BlockSpec((group_rows, LANES), here),
        whole(picks),
        whole(router),
        whole(first),
        whole(down),
    ] + [pl.BlockSpec(memory_space=pl.ANY)] * len(earlier)
    flops = 2 * steps * group_rows * width * 5 * hidden_all
    return pl.pallas_call(
        lambda *refs: expert_kernel(tp_count, expert_count, *refs),
        grid_spec=pltpu.PrefetchScalarGridSpec(
            num_scalar_prefetch=1,
            grid=(steps,),
            in_specs=in_specs,
            out_specs=[pl.BlockSpec((group_rows, width + LANES), fixed)] * 2
            + [
                pl.BlockSpec((group_rows, 2 * hidden_all), here),
                pl.BlockSpec((group_rows, hidden_all), here),
            ],
            scratch_shapes=[
                pltpu.VMEM((segments, group_rows, LANES), F32),
                pltpu.VMEM((group_rows, LANES), F32),
                pltpu.VMEM((group_rows, hidden_all), F32),
            ],
        ),
        out_shape=[jax.ShapeDtypeStruct((group_rows, width + LANES), BF16)] * 2
        + [
            jax.ShapeDtypeStruct((span_rows, 2 * hidden_all), BF16),
            jax.ShapeDtypeStruct((span_rows, hidden_all), BF16),
        ],
        input_output_aliases={8 + i: 2 + i for i in range(len(earlier))},
        compiler_params=pltpu.CompilerParams(vmem_limit_bytes=58 << 20),
        cost_estimate=pl.CostEstimate(
            flops=flops,
            bytes_accessed=2 * (first.size + down.size + steps * group_rows * (3 * width + 3 * hidden_all)),
            transcendentals=steps * group_rows * hidden_all,
        ),
        name="experts",
    )(jnp.stack([*groups, tp_index]).astype(jnp.int32), rows, upstream, mask, picks, router, first, down, *earlier)


def body(
    layer_input,
    cotangent,
    lengths,
    seq_order,
    routes,
    query_weight,
    key_weight,
    value_weight,
    mixing_weight,
    heads_bias,
    entry_gain,
    middle_gain,
    router_weight,
    shared_switch,
    shared_gate,
    shared_up,
    shared_down,
    expert_gate,
    expert_up,
    expert_down,
):
    tp_count = lax.axis_size("tp")
    ep_count = lax.axis_size("ep")
    dp_count = lax.axis_size("dp")
    part_count = dp_count * ep_count
    tp_index = lax.axis_index("tp")
    ep_index = lax.axis_index("ep")
    own_rows, width = layer_input.shape
    group_rows = own_rows * tp_count
    span_rows = group_rows * ep_count
    slice_rows = query_weight.shape[0]
    head_cols = query_weight.shape[1]
    head_count = head_cols // HD
    local_experts = expert_gate.shape[0]
    expert_count = router_weight.shape[1]
    hidden = expert_gate.shape[2]
    shared_hidden = shared_gate.shape[1] // ep_count
    segments = local_experts + 1
    seg = -(-max(hidden, shared_hidden) // LANES) * LANES

    span_lengths = jnp.take(
        lengths,
        lax.dynamic_slice_in_dim(seq_order, lax.axis_index("dp") * ep_count, ep_count, 0),
    )
    length = span_lengths[ep_index]
    own_keep = ((tp_index * own_rows + jnp.arange(own_rows)) < length).astype(F32)[:, None]
    block_of = jnp.arange(group_rows) // own_rows
    position = ((tp_index - block_of) % tp_count) * own_rows + jnp.arange(group_rows) % own_rows

    span_keep = (jnp.arange(group_rows)[None, :] < span_lengths[:, None]).reshape(span_rows, 1)
    lanes = jnp.arange(LANES)[None, :]
    column_of = jnp.concatenate(
        [ep_index * local_experts + jnp.arange(local_experts), jnp.array([expert_count])]
    )
    half = LANES // 2
    picks = jnp.concatenate([column_of, column_of + half])[:, None] == lanes
    picks = picks.astype(F32)

    bias_rows = heads_bias.size
    small = jnp.concatenate(
        [
            router_weight,
            shared_switch[:, None],
            entry_gain[:, None],
            middle_gain[:, None],
        ],
        axis=1,
    )
    bias_depth = -(-bias_rows // slice_rows)
    bias_cols = jnp.pad(heads_bias.reshape(-1), (0, bias_depth * slice_rows - bias_rows))
    bias_cols = bias_cols.reshape(bias_depth, slice_rows).T
    route_depth = -(-routes.size // slice_rows)
    route_cols = jnp.pad(routes.reshape(-1), (0, route_depth * slice_rows - routes.size))
    route_cols = route_cols.reshape(route_depth, slice_rows).T.astype(BF16)
    small = jnp.concatenate([small, bias_cols, route_cols], axis=1)
    small = jnp.pad(small, ((0, 0), (0, LANES - small.shape[1])))
    dense_own = jnp.concatenate(
        [query_weight, key_weight, value_weight, small], axis=1
    )
    input_blocks = gather_blocks(layer_input, "tp")
    dense_own = after(dense_own, input_blocks[1])
    dense_full = lax.all_gather(dense_own, ("dp", "ep"), axis=0, tiled=True)
    in_weight = dense_full[:, : 3 * head_cols]
    small_full = dense_full[:, 3 * head_cols :]
    out_weight = lax.all_gather(
        after(mixing_weight, dense_full), ("dp", "ep"), axis=1, tiled=True
    )
    small_rows = small_full[:, : expert_count + 3].astype(F32).T
    entry_full = small_rows[expert_count + 1][None]
    middle_full = small_rows[expert_count + 2][None]
    bias_full = small_full[:, expert_count + 3 : expert_count + 3 + bias_depth]
    bias_full = bias_full.reshape(part_count, slice_rows, bias_depth).transpose(0, 2, 1)
    bias_full = bias_full.reshape(part_count, -1)[:, :bias_rows]
    bias_full = bias_full.reshape((part_count,) + heads_bias.shape).transpose(1, 2, 0, 3)
    bias_full = bias_full.reshape(1, 3 * head_cols).astype(F32)

    route_at = expert_count + 3 + bias_depth
    span_routes = lax.dynamic_slice_in_dim(
        small_full[:, route_at : route_at + route_depth],
        lax.axis_index("dp") * ep_count * slice_rows,
        ep_count * slice_rows,
        0,
    )
    span_routes = span_routes.reshape(ep_count, slice_rows, route_depth).transpose(0, 2, 1)
    span_routes = span_routes.reshape(ep_count, -1)[:, : routes.size].reshape(span_rows, TOP)
    named = lanes == expert_count
    for k in range(TOP):
        named = named | (lanes == span_routes[:, k : k + 1].astype(jnp.int32))
    span_mask = (named & span_keep).astype(BF16)

    grad_blocks = gather_blocks(after(cotangent, input_blocks), "tp")
    input_values = jnp.concatenate(input_blocks, axis=0)

    def to_owners(matrix):
        return matrix.reshape(ep_count, shared_hidden, slice_rows)

    shared_own = jnp.concatenate(
        [to_owners(shared_gate.T), to_owners(shared_up.T), to_owners(shared_down)], axis=1
    )
    shared_own = after(shared_own, dense_full)
    shared_span = lax.all_to_all(shared_own, "ep", split_axis=0, concat_axis=0, tiled=True)
    freqs = THETA ** (-(jnp.arange(HD // 2).astype(F32) * 2.0) / HD)
    angles = position.astype(F32)[:, None] * freqs[None, :]
    angles = jnp.concatenate([angles, angles], axis=-1)
    cosine = jnp.cos(angles)[:, None, :]
    sine = jnp.sin(angles)[:, None, :]
    input_values = after(input_values, picks, cosine, sine).astype(F32)
    entry_unit, entry_inverse = norm_parts(input_values)
    entry_normed = (entry_unit * entry_full).astype(BF16)
    in_lin = dot_nn(entry_normed, in_weight) + bias_full
    query_heads = in_lin[:, :head_cols].reshape(group_rows, head_count, HD)
    key_heads = in_lin[:, head_cols : 2 * head_cols].reshape(group_rows, head_count, HD)
    query_rot = (query_heads * cosine + rotate(query_heads) * sine).astype(BF16)
    key_rot = (key_heads * cosine + rotate(key_heads) * sine).astype(BF16)
    value_heads = in_lin[:, 2 * head_cols :].astype(BF16).reshape(group_rows, head_count, HD)
    score_scale = HD ** (-0.5)
    causal = position[:, None] >= position[None, :]

    def score_matrix():
        raw_scores = jnp.einsum("qhd,khd->hqk", query_rot, key_rot, preferred_element_type=F32)
        return jnp.where(causal[None], raw_scores * score_scale, -1e30)

    scores = score_matrix()
    top_score = jnp.max(scores, axis=-1, keepdims=True)
    log_total = top_score + jnp.log(jnp.sum(jnp.exp(scores - top_score), axis=-1, keepdims=True))
    attn_probs = jnp.exp(scores - log_total).astype(BF16)
    context = jnp.einsum("hqk,khd->qhd", attn_probs, value_heads, preferred_element_type=F32)
    context_low = context.astype(BF16).reshape(group_rows, head_cols)
    head_blocks = split_rows(dot_nn(context_low, out_weight).astype(BF16), tp_count)
    attention_parts = send_blocks(head_blocks, "tp")

    shared_span = after(shared_span, head_blocks)
    if dp_count == 2:
        shared_other = swapped(shared_span, "dp", 1)
        shared_parts = in_order(shared_span, shared_other, lax.axis_index("dp"), 1)
    else:
        shared_parts = lax.all_gather(shared_span, "dp", axis=0, tiled=True)
    shared_parts = shared_parts.reshape(part_count, 3, shared_hidden, slice_rows)
    shared_parts = shared_parts.transpose(1, 2, 0, 3).reshape(3, shared_hidden, width)

    def stack_hidden(expert_rows, shared_rows):
        padded = [jnp.pad(rows, ((0, seg - rows.shape[0]), (0, 0))) for rows in expert_rows]
        padded.append(jnp.pad(shared_rows, ((0, seg - shared_hidden), (0, 0))))
        return padded

    gate_rows = stack_hidden([expert_gate[j].T for j in range(local_experts)], shared_parts[0])
    up_rows = stack_hidden([expert_up[j].T for j in range(local_experts)], shared_parts[1])
    down_rows = stack_hidden([expert_down[j] for j in range(local_experts)], shared_parts[2])
    first_weight = jnp.concatenate(
        [rows for pair in zip(gate_rows, up_rows) for rows in pair], axis=0
    )
    down_weight = jnp.concatenate(down_rows, axis=0)

    grad_blocks = after(grad_blocks, head_blocks)
    group_upstream = jnp.concatenate(grad_blocks, axis=0)
    near = swapped(group_upstream, "ep", 2)

    attention_parts = after(attention_parts, near)
    if dp_count == 2:
        attention_parts = after(attention_parts, shared_other)
    attention_own = add_up([head_blocks[0], *attention_parts])
    hidden_state = input_values[:own_rows] + own_keep * attention_own
    middle_unit, middle_inverse = norm_parts(hidden_state)
    middle_normed = (middle_unit * middle_full).astype(BF16)

    span_normed = lax.all_gather(middle_normed, ("ep", "tp"), axis=0, tiled=True)
    sibling, far = swapped(group_upstream, "ep", 1), swapped(near, "ep", 1)

    def upstream_moves(_, place, turn):
        moves = []
        for k in range(4):
            for j in range(tp_count):
                block = (place ^ k) * tp_count + lax.rem(turn - j + tp_count, tp_count)
                start = pl.multiple_of(block * own_rows, own_rows)
                moves.append((k, pl.ds(j * own_rows, own_rows), 0, pl.ds(start, own_rows)))
        return moves

    upstream = move_blocks(
        upstream_moves,
        [jax.ShapeDtypeStruct((span_rows, width), BF16)],
        [group_upstream, sibling, near, far],
        "order_rows",
    )[0]

    own_logits = dot_nn(middle_normed, small_full)
    expert_probs = jax.nn.softmax(own_logits[:, :expert_count], axis=-1)
    switch_value = jax.nn.sigmoid(own_logits[:, expert_count : expert_count + 1])
    own_routes = lax.dynamic_slice_in_dim(routes, tp_index * own_rows, own_rows, 0)
    route_mask = jnp.any(
        own_routes[:, :, None] == jnp.arange(expert_count)[None, None, :], axis=1
    ).astype(F32)

    first_weight, down_weight = after((first_weight, down_weight), middle_normed)
    span_mask = after(span_mask, expert_probs, switch_value, route_mask)
    small_rows_low = small_full.T
    shared_operands = (span_normed, upstream, span_mask, picks, small_rows_low, first_weight, down_weight)
    sibling_back, chip_back, *made = run_experts(
        (ep_index ^ 3, ep_index ^ 2), tp_index, tp_count, expert_count, *shared_operands, ()
    )
    chip_sum = add_up([chip_back, swapped(sibling_back, "ep", 1)]).astype(BF16)
    from_chip = swapped(chip_sum, "ep", 2)
    sibling_back, group_back, first_grad, hidden_gated = run_experts(
        (after(ep_index ^ 1, chip_sum), ep_index),
        tp_index,
        tp_count,
        expert_count,
        *shared_operands,
        made,
    )
    from_core = [swapped(block, "ep", 1) for block in split_rows(sibling_back, tp_count)]
    down_grad = dot_tn(hidden_gated, upstream).astype(BF16)

    def last_moves(*_):
        return [
            (0, pl.ds(j * seg, hidden), 0, pl.ds(j * hidden, hidden)) for j in range(local_experts)
        ]

    last_own = move_blocks(
        last_moves,
        [jax.ShapeDtypeStruct((local_experts * hidden, width), BF16)],
        [down_grad],
        "down_rows",
    )[0]
    last_other = swapped_or_none(last_own, "dp")
    from_core = after(from_core, last_own)
    back_blocks = [
        add_up(blocks)
        for blocks in zip(
            split_rows(group_back, tp_count), from_core, split_rows(from_chip, tp_count)
        )
    ]
    back_blocks = [back_blocks[0]] + [block.astype(BF16) for block in back_blocks[1:]]
    back_parts = send_blocks(back_blocks, "tp")

    first_grad = after(first_grad, back_blocks)
    first_weight_grad = dot_tn(first_grad, span_normed).astype(BF16)
    shared_size = width // dp_count

    def first_moves(place, *_):
        moves = [
            (0, pl.ds((2 * j + part) * seg, hidden), part, pl.ds(j * hidden, hidden))
            for part in range(2)
            for j in range(local_experts)
        ]
        starts = (place, 1 - place) if dp_count == 2 else (0, 0)
        for k, start in enumerate(starts):
            columns = pl.ds(0, width)
            if dp_count == 2:
                columns = pl.ds(pl.multiple_of(start * shared_size, LANES), shared_size)
            for part, (array, base) in enumerate(
                ((0, 2 * local_experts * seg), (0, (2 * local_experts + 1) * seg), (1, local_experts * seg))
            ):
                moves.append(
                    (
                        array,
                        (pl.ds(base, shared_hidden), columns),
                        2 + k,
                        pl.ds(part * shared_hidden, shared_hidden),
                    )
                )
        return moves

    shared_shape = (3 * shared_hidden, shared_size if dp_count == 2 else width)
    *first_own, shared_kept, shared_given = move_blocks(
        first_moves,
        [jax.ShapeDtypeStruct((local_experts * hidden, width), BF16)] * 2
        + [jax.ShapeDtypeStruct(shared_shape, BF16)] * 2,
        [first_weight_grad, down_grad],
        "first_rows",
    )
    first_other = [swapped_or_none(part, "dp") for part in first_own]
    hidden_gated = after(hidden_gated, first_own)
    branch = dot_nn(hidden_gated, down_weight).astype(BF16)
    branch_terms = lax.all_to_all(
        branch.reshape(ep_count, group_rows, width), "ep", split_axis=0, concat_axis=0, tiled=True
    )
    back_parts = after(back_parts, branch, shared_kept, shared_given)
    if dp_count == 2:
        back_parts = after(back_parts, last_other)

    state_grad, attention_grad_own, router_part, middle_part = run_own(
        expert_count,
        [back_blocks[0], *back_parts],
        (expert_probs, route_mask, switch_value, own_keep),
        small_rows_low,
        middle_unit,
        middle_inverse,
        middle_normed,
        cotangent,
    )
    router_part = router_part[: expert_count + 1]
    attention_grad_blocks = gather_blocks(attention_grad_own, "tp")

    if dp_count == 2:
        attention_grad_blocks = after(attention_grad_blocks, first_other[0])
    attention_grad = jnp.concatenate(attention_grad_blocks, axis=0)
    grads_other = swapped_or_none(shared_given, "dp")

    mixing_grad = dot_tn(context_low, attention_grad).astype(BF16)
    mixing_sum = lax.psum_scatter(mixing_grad, ("dp", "ep"), scatter_dimension=1, tiled=True)
    context_grad = dot_nt(attention_grad, out_weight)
    context_grad = context_grad.astype(BF16).reshape(group_rows, head_count, HD)
    probs_again = jnp.exp(score_matrix() - log_total)
    probs_low = probs_again.astype(BF16)
    value_grad = jnp.einsum("hqk,qhd->khd", probs_low, context_grad, preferred_element_type=F32)
    value_grad = value_grad.astype(BF16).reshape(group_rows, head_cols)
    prob_grads = jnp.einsum("qhd,khd->hqk", context_grad, value_heads, preferred_element_type=F32)
    row_delta = jnp.sum(probs_again * prob_grads, axis=-1, keepdims=True)
    score_grads = (probs_again * (prob_grads - row_delta)).astype(BF16)
    query_rot_grad = (
        jnp.einsum("hqk,khd->qhd", score_grads, key_rot, preferred_element_type=F32) * score_scale
    )
    key_rot_grad = (
        jnp.einsum("hqk,qhd->khd", score_grads, query_rot, preferred_element_type=F32) * score_scale
    )
    query_grad = (query_rot_grad * cosine + unrotate(query_rot_grad * sine)).astype(BF16)
    key_grad = (key_rot_grad * cosine + unrotate(key_rot_grad * sine)).astype(BF16)
    query_grad = after(query_grad, mixing_grad)
    in_grad = jnp.concatenate(
        [query_grad.reshape(group_rows, head_cols), key_grad.reshape(group_rows, head_cols), value_grad],
        axis=1,
    )
    branch_blocks = []
    for j in range(tp_count):
        start = ((tp_index - j) % tp_count) * own_rows
        rows = lax.dynamic_slice_in_dim(branch_terms, start, own_rows, 1)
        branch_blocks.append(jnp.sum(rows.astype(F32), axis=0))
    branch_blocks = [branch_blocks[0]] + [block.astype(BF16) for block in branch_blocks[1:]]
    branch_parts = send_blocks(branch_blocks, "tp")
    in_grad = after(in_grad, branch_blocks)
    bias_grad = jnp.sum(in_grad.astype(F32), axis=0)
    entry_part = dot_nt(in_grad, in_weight)
    entry_blocks = split_rows(entry_part.astype(BF16), tp_count)
    entry_parts = send_blocks(entry_blocks, "tp")
    if dp_count == 2:
        shared_mine = add_up([shared_kept, grads_other]).astype(BF16)
    else:
        shared_mine = lax.psum_scatter(shared_kept, "dp", scatter_dimension=1, tiled=True)
    shared_mine = shared_mine.reshape(3 * shared_hidden, ep_count, slice_rows).transpose(1, 0, 2)
    shared_back = lax.all_to_all(shared_mine, "ep", split_axis=0, concat_axis=0, tiled=True)
    shared_back = shared_back.reshape(ep_count, 3, shared_hidden, slice_rows).astype(F32)
    last_sum = whole_sum(last_own, last_other, "dp").reshape(local_experts, hidden, width)
    first_sum = [whole_sum(first_own[0], first_other[0], "dp")]
    entry_parts = after(entry_parts, branch_parts, shared_mine, last_sum, first_sum)
    if dp_count == 2:
        first_other[1] = after(first_other[1], entry_parts)
    first_sum.append(whole_sum(first_own[1], first_other[1], "dp"))
    first_sum = [part.reshape(local_experts, hidden, width) for part in first_sum]
    entry_own = add_up([entry_blocks[0], *entry_parts])
    input_gradient = state_grad + norm_back(
        entry_own, entry_full, entry_unit[:own_rows], entry_inverse[:own_rows]
    )

    entry_gain_part = jnp.sum(entry_part * entry_unit, axis=0, keepdims=True)
    small_part = jnp.concatenate([router_part, middle_part, entry_gain_part], axis=0)
    bias_part = bias_grad.reshape(3, head_count, part_count, -1).transpose(2, 0, 1, 3)
    bias_part = bias_part.reshape(part_count, bias_rows)
    bias_part = jnp.pad(bias_part, ((0, 0), (0, bias_depth * slice_rows - bias_rows)))
    bias_part = bias_part.reshape(part_count, bias_depth, slice_rows).transpose(1, 0, 2)
    bias_part = bias_part.reshape(bias_depth, width)
    small_part = jnp.concatenate([small_part, bias_part], axis=0)
    small_high, small_low = split_pair(small_part)
    small_count = small_part.shape[0]
    small_cols = jnp.concatenate(
        [
            jnp.pad(small_high, ((0, half - small_count), (0, 0))),
            jnp.pad(small_low, ((0, half - small_count), (0, 0))),
        ],
        axis=0,
    ).T
    dense_grad = jnp.concatenate(
        [
            dot_tn(entry_normed, in_grad).astype(BF16),
            small_cols,
        ],
        axis=1,
    )
    if dp_count == 2:
        dense_grad = after(dense_grad, grads_other)
    dense_grad = after(dense_grad, branch_parts[0], branch_parts[-1])
    dense_sum = lax.psum_scatter(
        dense_grad, ("dp", "ep"), scatter_dimension=0, tiled=True
    ).astype(F32)
    small_sum = dense_sum[:, 3 * head_cols : 3 * head_cols + half] + dense_sum[:, 3 * head_cols + half :]
    tp_sum = ordered_sum(small_sum[:, : expert_count + 3].T, "tp")
    bias_sum = small_sum[:, expert_count + 3 : expert_count + 3 + bias_depth]
    bias_sum = bias_sum.T.reshape(-1)[:bias_rows].reshape(heads_bias.shape)

    layer_output = (hidden_state + add_up([branch_blocks[0], *branch_parts])).astype(BF16)
    def by_columns(rows):
        return rows.transpose(2, 0, 1).reshape(slice_rows, ep_count * shared_hidden)

    return (
        layer_output,
        input_gradient,
        dense_sum[:, :head_cols],
        dense_sum[:, head_cols : 2 * head_cols],
        dense_sum[:, 2 * head_cols : 3 * head_cols],
        mixing_sum.astype(F32),
        bias_sum,
        tp_sum[expert_count + 2],
        tp_sum[expert_count + 1],
        tp_sum[:expert_count].T,
        tp_sum[expert_count],
        by_columns(shared_back[:, 0]),
        by_columns(shared_back[:, 1]),
        shared_back[:, 2].reshape(ep_count * shared_hidden, slice_rows),
        first_sum[0].transpose(0, 2, 1),
        first_sum[1].transpose(0, 2, 1),
        last_sum,
    )


def solution(mesh):
    rows = P(("dp", "ep", "tp"), None)
    parts = P(("dp", "ep"))
    in_cols = P(("dp", "ep"), "tp")
    out_cols = P("tp", ("dp", "ep"))
    weights = (
        in_cols,
        in_cols,
        in_cols,
        out_cols,
        P(None, "tp", ("dp", "ep")),
        parts,
        parts,
        P(("dp", "ep"), None),
        parts,
        in_cols,
        in_cols,
        out_cols,
        P("ep", None, "tp"),
        P("ep", None, "tp"),
        P("ep", "tp", None),
    )
    return jax.shard_map(
        body,
        mesh=mesh,
        in_specs=(rows, rows, P(), P(), P(("dp", "ep"), None)) + weights,
        out_specs=(rows, rows) + weights,
        check_vma=False,
    )
```
